32 devices in a mesh: dp: 8 (over y, x, core), head: 4 (over z).
Axes of the slice: x: 2, y: 2, z: 4, core: 2. Of those that a mesh axis runs over, the one named last changes fastest.
Arguments:
- latents: bfloat16 [12288, 1024], P('dp'), may hold values from -6 to 6
- media_tokens: bfloat16 [49152, 1024], P('dp'), may hold values from -6 to 6
- image_counts: int32 [64], replicated, may hold values from 1 to 5, 192 in all
- time_table: bfloat16 [5, 1024], replicated, may hold values from -3 to 3
- media_gain: float32 [1024], replicated, may hold values from 0.5 to 1.5
- media_bias: float32 [1024], replicated, may hold values from -1 to 1
- latent_gain: float32 [1024], replicated, may hold values from 0.5 to 1.5
- latent_bias: float32 [1024], replicated, may hold values from -1 to 1
- feed_gain: float32 [1024], replicated, may hold values from 0.5 to 1.5
- feed_bias: float32 [1024], replicated, may hold values from -1 to 1
- query_weight: bfloat16 [1024, 512], P('dp', 'head'), may hold values from -0.1875 to 0.1875
- key_weight: bfloat16 [1024, 512], P('dp', 'head'), may hold values from -0.1875 to 0.1875
- value_weight: bfloat16 [1024, 512], P('dp', 'head'), may hold values from -0.1875 to 0.1875
- out_weight: bfloat16 [512, 1024], P('head', 'dp'), may hold values from -1 to 1
- up_weight: bfloat16 [1024, 4096], P('dp', 'head'), may hold values from -0.1875 to 0.1875
- down_weight: bfloat16 [4096, 1024], P('head', 'dp'), may hold values from -0.09375 to 0.09375
- cotangent: bfloat16 [12288, 1024], P('dp', 'head'), may hold values from -6 to 6
Outputs:
- latents_out: float32 [12288, 1024], P('dp', 'head')
- latents_grad: float32 [12288, 1024], P('dp')
- time_grad: float32 [5, 1024], replicated
- media_gain_grad: float32 [1024], replicated
- media_bias_grad: float32 [1024], replicated
- latent_gain_grad: float32 [1024], replicated
- latent_bias_grad: float32 [1024], replicated
- feed_gain_grad: float32 [1024], replicated
- feed_bias_grad: float32 [1024], replicated
- query_grad: float32 [1024, 512], P('dp', 'head')
- key_grad: float32 [1024, 512], P('dp', 'head')
- value_grad: float32 [1024, 512], P('dp', 'head')
- out_grad: float32 [512, 1024], P('head', 'dp')
- up_grad: float32 [1024, 4096], P('dp', 'head')
- down_grad: float32 [4096, 1024], P('head', 'dp')
The draws below stay inside these ranges and needn't reach their ends.
Inputs may be any that keep to these rules, and one draw needn't show every extreme that they name: `image_counts`: each sample holds 1 to 5 images, the counts sum to 192, and some sample holds exactly 5.
All inputs are finite; a program needn't handle non-finite values.
Results may differ from the reference program's by a relative error of at most 0.017.
Values may be sent and summed in bfloat16 or wider, within the bound.
No kernel may reach another device: no remote copies, remote signals or barrier semaphores. Data moves between devices by JAX's collectives and lax.ppermute only.
A program may use at most 192 MiB of HBM per device.

```python
import math
import jax
import jax.numpy as jnp
import numpy as np
from jax import lax

D = 1024
HEADS = 8
DH = 64
INNER = 512
FF = 4096
LAT = 64
PATCH = 256
MAX_MEDIA = 5
IMAGES = 192
SAMPLES = 64
N_HEAD = 4


def level_of(key, dims, shards, least, top_value):
    loudness, own = 1.0, jax.random.fold_in(key, 6)
    for axis_at, blocks in shards:
        steps = jnp.exp(jax.random.uniform(jax.random.fold_in(own, axis_at), (blocks,), jnp.float32, least / len(shards), top_value / len(shards)))
        loudness = loudness * jnp.repeat(steps, dims[axis_at] // blocks).reshape([-1 if axis == axis_at else 1 for axis in range(len(dims))])
    return loudness


def profile(amount, total, most, slope):
    loads = [(1 << 20) // math.isqrt(grade ** slope) + 1 for grade in range(2, amount + 1)]
    surplus, given = total - most - (amount - 1), [1] * (amount - 1)
    while surplus > 0:
        movable = [i for i in range(amount - 1) if given[i] < most]
        pool, budget = sum([loads[i] for i in movable]), surplus
        for i in movable:
            addition = min(most - given[i], max(1, budget * loads[i] // pool), surplus)
            given[i] = given[i] + addition
            surplus = surplus - addition
    return np.array([most] + given)


def uneven(stream_key, number_of, total, bound, skew):
    if number_of == 2:
        one = jax.random.randint(stream_key, (), max(1, total - bound), min(bound, total - 1) + 1)
        return jnp.stack([one, total - one])
    sizes = jnp.asarray(profile(number_of, total, bound, skew), jnp.int32)
    twos = (number_of - 1) // 2
    giver, sink = sizes[1:1 + 2 * twos:2], sizes[2:2 + 2 * twos:2]
    margin = jnp.minimum(giver - 1, bound - sink)
    moved = jax.random.randint(jax.random.fold_in(stream_key, 1), (twos,), 0, 1 << 20) % (margin + 1)
    sizes = sizes.at[1:1 + 2 * twos:2].set(giver - moved).at[2:2 + 2 * twos:2].set(sink + moved)
    return sizes[jax.random.permutation(jax.random.fold_in(stream_key, 2), number_of)]


def noise(own_key, dims, deviation, bound, split=(), held_as=jnp.bfloat16):
    array = deviation * jax.random.normal(own_key, dims, jnp.float32)
    if split:
        array = array * level_of(own_key, dims, split, -0.22, 0.18)
    return jnp.clip(array, -bound, bound).astype(held_as)


def setup_inputs(seed: int = 0) -> dict:
    streams_of = jax.random.split(jax.random.key(seed), 18)
    return {
        "latents": noise(streams_of[0], (IMAGES * LAT, D), 1.0, 6.0, ((0, 8),)),
        "media_tokens": noise(streams_of[1], (IMAGES * PATCH, D), 1.0, 6.0, ((0, 8),)),
        "image_counts": uneven(streams_of[2], SAMPLES, IMAGES, MAX_MEDIA, 1).astype(jnp.int32),
        "time_table": noise(streams_of[3], (MAX_MEDIA, D), 0.5, 3.0),
        "media_gain": jnp.clip(1.0 + 0.1 * jax.random.normal(streams_of[4], (D,), jnp.float32), 0.5, 1.5),
        "media_bias": noise(streams_of[5], (D,), 0.2, 1.0, (), jnp.float32),
        "latent_gain": jnp.clip(1.0 + 0.1 * jax.random.normal(streams_of[6], (D,), jnp.float32), 0.5, 1.5),
        "latent_bias": noise(streams_of[7], (D,), 0.2, 1.0, (), jnp.float32),
        "feed_gain": jnp.clip(1.0 + 0.1 * jax.random.normal(streams_of[8], (D,), jnp.float32), 0.5, 1.5),
        "feed_bias": noise(streams_of[9], (D,), 0.2, 1.0, (), jnp.float32),
        "query_weight": noise(streams_of[10], (D, INNER), D ** -0.5, 0.1875, ((0, 8), (1, 4))),
        "key_weight": noise(streams_of[11], (D, INNER), D ** -0.5, 0.1875, ((0, 8), (1, 4))),
        "value_weight": noise(streams_of[12], (D, INNER), D ** -0.5, 0.1875, ((0, 8), (1, 4))),
        "out_weight": noise(streams_of[13], (INNER, D), (INNER // 16) ** -0.5, 1.0, ((0, 4), (1, 8))),
        "up_weight": noise(streams_of[14], (D, FF), D ** -0.5, 0.1875, ((0, 8), (1, 4))),
        "down_weight": noise(streams_of[15], (FF, D), FF ** -0.5, 0.09375, ((0, 4), (1, 8))),
        "cotangent": noise(streams_of[16], (IMAGES * LAT, D), 1.0, 6.0, ((0, 8), (1, 4))),
    }


@jax.custom_vjp
def low(v):
    return lax.optimization_barrier(v.astype(jnp.bfloat16)).astype(jnp.float32)

@jax.custom_vjp
def low_back(v):
    return v

def low_keep(v):
    return (low(v), None)

def low_pass(kept, grad):
    return (grad,)

def back_keep(v):
    return (v, None)

def back_low(kept, grad):
    return (low(grad),)
low.defvjp(low_keep, low_pass)
low_back.defvjp(back_keep, back_low)
epsilon = 1e-05
highest = lax.Precision.HIGHEST

def layer_norm(values_in, norm_gain, norm_bias):
    centre = lax.optimization_barrier(jnp.mean(values_in, axis=-1, keepdims=True))
    shifted = values_in - centre
    spread = lax.optimization_barrier(jnp.mean(shifted * shifted, axis=-1, keepdims=True))
    return shifted * lax.rsqrt(spread + epsilon) * norm_gain + norm_bias

def gelu_exact(up_proj):
    return up_proj * 0.5 * (1.0 + lax.erf(up_proj * 0.5 ** 0.5))

def slot_table_of(image_counts):
    counts_sum = jnp.cumsum(image_counts).astype(jnp.int32)
    starts = (counts_sum - image_counts).astype(jnp.int32)
    image_index = jnp.arange(IMAGES, dtype=jnp.int32)
    latest = lax.optimization_barrier(jnp.max(jnp.where(starts[None, :] <= image_index[:, None], starts[None, :], 0), axis=1)).astype(jnp.int32)
    media_slot = (image_index - latest).astype(jnp.int32)
    return (media_slot[:, None] == jnp.arange(MAX_MEDIA, dtype=jnp.int32)[None, :]).astype(jnp.float32)

def attend_block(query_block, key_block, value_block):
    image_count = query_block.shape[0]
    query_heads = query_block.reshape(image_count, LAT, HEADS, DH)
    key_heads = key_block.reshape(image_count, PATCH + LAT, HEADS, DH)
    value_heads = value_block.reshape(image_count, PATCH + LAT, HEADS, DH)
    scores = low_back(jnp.einsum('bqhe,bkhe->bhqk', query_heads, key_heads, precision=highest) * DH ** (-0.5))
    row_top = lax.optimization_barrier(jnp.max(scores, axis=-1, keepdims=True))
    expd = jnp.exp(scores - row_top)
    probability = low(expd / lax.optimization_barrier(jnp.sum(expd, axis=-1, keepdims=True)))
    mixed_heads = jnp.einsum('bhqk,bkhe->bqhe', probability, value_heads, precision=highest)
    return mixed_heads.reshape(image_count, LAT, INNER)

def attend_parts(parts):
    return jax.checkpoint(attend_block)(parts[0], parts[1], parts[2])

def forward(latents_f, time_f, media_gain, media_bias, latent_gain, latent_bias, feed_gain, feed_bias, query_weight, key_weight, value_weight, out_weight, up_weight, down_weight, media_f, slot_table):
    per_image = jnp.dot(slot_table, time_f, precision=highest)
    media_sum = media_f.reshape(IMAGES, PATCH, D) + per_image[:, None, :]
    media_norm = low(layer_norm(media_sum, media_gain, media_bias))
    latent_norm = low(layer_norm(latents_f, latent_gain, latent_bias)).reshape(IMAGES, LAT, D)
    kv_input = jnp.concatenate([media_norm, latent_norm], axis=1)
    query = low_back(low(jnp.einsum('ild,de->ile', latent_norm, query_weight, precision=highest)))
    key = low_back(low(jnp.einsum('ikd,de->ike', kv_input, key_weight, precision=highest)))
    value = low_back(low(jnp.einsum('ikd,de->ike', kv_input, value_weight, precision=highest)))
    block_images = math.gcd(IMAGES, 8)
    blocks = IMAGES // block_images
    mixed = lax.map(attend_parts, (query.reshape(blocks, block_images, LAT, INNER), key.reshape(blocks, block_images, PATCH + LAT, INNER), value.reshape(blocks, block_images, PATCH + LAT, INNER)))
    mixed = low_back(low(mixed.reshape(IMAGES * LAT, INNER)))
    group_cols = INNER // N_HEAD
    attention = jnp.zeros((IMAGES * LAT, D), jnp.float32)
    for group in range(N_HEAD):
        part_term = jnp.dot(mixed[:, group * group_cols:(group + 1) * group_cols], out_weight[group * group_cols:(group + 1) * group_cols], precision=highest)
        attention = attention + low(part_term)
    attention = low_back(attention)
    hidden = latents_f + attention
    feed_norm = low(layer_norm(hidden, feed_gain, feed_bias))
    up_proj = low_back(jnp.dot(feed_norm, up_weight, precision=highest))
    activation = low(gelu_exact(up_proj))
    group_units = FF // N_HEAD
    result = hidden
    for group in range(N_HEAD):
        part_term = jnp.dot(activation[:, group * group_units:(group + 1) * group_units], down_weight[group * group_units:(group + 1) * group_units], precision=highest)
        result = result + low(part_term)
    return result

def reference(latents, media_tokens, image_counts, time_table, media_gain, media_bias, latent_gain, latent_bias, feed_gain, feed_bias, query_weight, key_weight, value_weight, out_weight, up_weight, down_weight, cotangent):
    slot_table = slot_table_of(image_counts)
    media_f = media_tokens.astype(jnp.float32)
    primals = (latents.astype(jnp.float32), time_table.astype(jnp.float32), media_gain.astype(jnp.float32), media_bias.astype(jnp.float32), latent_gain.astype(jnp.float32), latent_bias.astype(jnp.float32), feed_gain.astype(jnp.float32), feed_bias.astype(jnp.float32), query_weight.astype(jnp.float32), key_weight.astype(jnp.float32), value_weight.astype(jnp.float32), out_weight.astype(jnp.float32), up_weight.astype(jnp.float32), down_weight.astype(jnp.float32))

    def wrapped(*params):
        return forward(*params, media_f, slot_table)
    result, pullback = jax.vjp(wrapped, *primals)
    grads = pullback(cotangent.astype(jnp.float32))
    return (result, grads[0], grads[1], grads[2], grads[3], grads[4], grads[5], grads[6], grads[7], grads[8], grads[9], grads[10], grads[11], grads[12], grads[13])
```

```python
import math

import jax
import jax.numpy as jnp
from jax import lax
from jax.experimental import pallas as pl
from jax.experimental.pallas import tpu as pltpu
from jax.sharding import PartitionSpec as P

D = 1024
DH = 64
LAT = 64
PATCH = 256
MAX_MEDIA = 5
GROUP = 4

epsilon = 1e-05
highest = lax.Precision.HIGHEST
bf16 = jnp.bfloat16
f32 = jnp.float32


def mm(left, right):
    return lax.dot_general(left, right, (((1,), (0,)), ((), ())), preferred_element_type=f32)


def mm_tn(left, right):
    return lax.dot_general(left, right, (((0,), (0,)), ((), ())), preferred_element_type=f32)


def mm_nt(left, right):
    return lax.dot_general(left, right, (((1,), (1,)), ((), ())), preferred_element_type=f32)


def norm_stats(values_in):
    centre = jnp.mean(values_in, axis=-1, keepdims=True)
    shifted = values_in - centre
    spread = jnp.mean(shifted * shifted, axis=-1, keepdims=True)
    inverse = lax.rsqrt(spread + epsilon)
    return (shifted * inverse, inverse)


def norm_back(grad_in, scaled, inverse, norm_gain):
    weighted = grad_in * norm_gain
    return inverse * (
        weighted
        - jnp.mean(weighted, axis=-1, keepdims=True)
        - scaled * jnp.mean(weighted * scaled, axis=-1, keepdims=True)
    )


def gelu_exact(up_proj):
    return up_proj * 0.5 * (1.0 + lax.erf(up_proj * 0.5**0.5))


def gelu_slope(up_proj):
    normal_cdf = 0.5 * (1.0 + lax.erf(up_proj * 0.5**0.5))
    normal_pdf = jnp.exp(-0.5 * up_proj * up_proj) * (2.0 * math.pi) ** (-0.5)
    return normal_cdf + up_proj * normal_pdf


def own_blocks():
    width = GROUP * DH
    rows = lax.broadcasted_iota(jnp.int32, (GROUP * LAT, width), 0) // LAT
    cols = lax.broadcasted_iota(jnp.int32, (GROUP * LAT, width), 1) // DH
    return rows == cols


def spread_heads(block, mask):
    return jnp.where(mask, jnp.concatenate([block] * GROUP, axis=0), jnp.zeros((), block.dtype))


def gather_heads(blocks, mask):
    kept = jnp.where(mask, blocks, 0.0)
    return sum(kept[g * LAT : (g + 1) * LAT] for g in range(GROUP))


def soft_of(query_diag, keys):
    scores = mm_nt(query_diag, keys) * (DH**-0.5)
    expd = jnp.exp(scores - jnp.max(scores, axis=-1, keepdims=True))
    return expd / jnp.sum(expd, axis=-1, keepdims=True)


def attend_kernel(q_ref, km_ref, kl_ref, vm_ref, vl_ref, mixed_ref):
    mask = own_blocks()
    width = GROUP * DH
    for g in range(q_ref.shape[1] // width):
        cols = slice(g * width, (g + 1) * width)
        keys = jnp.concatenate([km_ref[:, cols], kl_ref[:, cols]], axis=0)
        values = jnp.concatenate([vm_ref[:, cols], vl_ref[:, cols]], axis=0)
        soft = soft_of(spread_heads(q_ref[:, cols], mask), keys)
        mixed_ref[:, cols] = gather_heads(mm(soft.astype(bf16), values), mask).astype(bf16)


def attend_back_kernel(
    q_ref, km_ref, kl_ref, vm_ref, vl_ref, dm_ref, dq_ref, dkm_ref, dkl_ref, dvm_ref, dvl_ref
):
    mask = own_blocks()
    width = GROUP * DH
    for g in range(q_ref.shape[1] // width):
        cols = slice(g * width, (g + 1) * width)
        keys = jnp.concatenate([km_ref[:, cols], kl_ref[:, cols]], axis=0)
        values = jnp.concatenate([vm_ref[:, cols], vl_ref[:, cols]], axis=0)
        query_diag = spread_heads(q_ref[:, cols], mask)
        mixed_diag = spread_heads(dm_ref[:, cols], mask)
        soft = soft_of(query_diag, keys)
        d_prob = mm_nt(mixed_diag, values)
        d_value = mm_tn(soft.astype(bf16), mixed_diag).astype(bf16)
        delta = jnp.sum(soft * d_prob, axis=-1, keepdims=True)
        d_scores = (soft * (d_prob - delta)).astype(bf16)
        d_query = gather_heads(mm(d_scores, keys), mask) * (DH**-0.5)
        d_key = (mm_tn(d_scores, query_diag) * (DH**-0.5)).astype(bf16)
        dq_ref[:, cols] = d_query.astype(bf16)
        dkm_ref[:, cols] = d_key[:PATCH]
        dkl_ref[:, cols] = d_key[PATCH:]
        dvm_ref[:, cols] = d_value[:PATCH]
        dvl_ref[:, cols] = d_value[PATCH:]


def image_spec(rows, cols, block_col=0):
    return pl.BlockSpec((rows, cols), lambda n: (n, block_col))


def attend(query, media_kv, latent_kv):
    inner = query.shape[1]
    images = query.shape[0] // LAT
    return pl.pallas_call(
        attend_kernel,
        grid=(images,),
        in_specs=[
            image_spec(LAT, inner),
            image_spec(PATCH, inner, 0),
            image_spec(LAT, inner, 0),
            image_spec(PATCH, inner, 1),
            image_spec(LAT, inner, 1),
        ],
        out_specs=image_spec(LAT, inner),
        out_shape=jax.ShapeDtypeStruct(query.shape, bf16),
        name="attend",
    )(query, media_kv, latent_kv, media_kv, latent_kv)


def attend_back(query, media_kv, latent_kv, d_mixed):
    inner = query.shape[1]
    images = query.shape[0] // LAT
    media_shape = jax.ShapeDtypeStruct((media_kv.shape[0], inner), bf16)
    latent_shape = jax.ShapeDtypeStruct(query.shape, bf16)
    return pl.pallas_call(
        attend_back_kernel,
        grid=(images,),
        in_specs=[
            image_spec(LAT, inner),
            image_spec(PATCH, inner, 0),
            image_spec(LAT, inner, 0),
            image_spec(PATCH, inner, 1),
            image_spec(LAT, inner, 1),
            image_spec(LAT, inner),
        ],
        out_specs=[
            image_spec(LAT, inner),
            image_spec(PATCH, inner),
            image_spec(LAT, inner),
            image_spec(PATCH, inner),
            image_spec(LAT, inner),
        ],
        out_shape=[latent_shape, media_shape, latent_shape, media_shape, latent_shape],
        name="attend_back",
    )(query, media_kv, latent_kv, media_kv, latent_kv, d_mixed)


def make_step(n_dp, n_head):
    def swap(block, bit):
        return lax.ppermute(block, "dp", [(j, j ^ bit) for j in range(n_dp)])

    def shift(block, step):
        return lax.ppermute(block, "head", [(j, (j + step) % n_head) for j in range(n_head)])

    def swap_head(block, bit):
        return lax.ppermute(block, "head", [(j, j ^ bit) for j in range(n_head)])

    ordered = [1 << b for b in range(1, n_dp.bit_length() - 1)]
    paths = (ordered, ordered[::-1])
    evens = list(range(0, n_dp, 2))
    places = evens + [m | 1 for m in evens]

    def to_own(values_in, me):
        size = D // n_dp
        parts = [lax.dynamic_slice_in_dim(values_in, (me ^ m) * size, size, 1) for m in places]
        return jnp.concatenate(parts, axis=1)

    def to_plain(values_in, me):
        size = D // n_dp
        parts = []
        for j in range(n_dp):
            m = me ^ j
            at = (m >> 1) + (m & 1) * (n_dp // 2)
            parts.append(lax.dynamic_slice_in_dim(values_in, at * size, size, 1))
        return jnp.concatenate(parts, axis=1)

    def gather(shard):
        columns = [shard] + [shift(shard, s) for s in range(1, n_head)]
        half = n_head // 2
        sides = []
        for bits, part in zip(paths, (columns[:half], columns[half:])):
            held = {0: jnp.concatenate(part, axis=1)}
            for bit in bits:
                for m in list(held):
                    held[m | bit] = swap(held[m], bit)
            sides.append(jnp.concatenate([held[m] for m in evens], axis=0))
        even = jnp.concatenate(sides, axis=1)
        return (even, swap(even, 1))

    def scatter(keep, send):
        arrived = swap(send, 1)
        total_rows, total_cols = keep.shape
        rows = total_rows // len(evens)
        half = total_cols // 2
        sides = []
        for bits, side in zip(paths, (0, 1)):
            held = {}
            for at, m in enumerate(evens):
                block = (slice(at * rows, (at + 1) * rows), slice(side * half, (side + 1) * half))
                held[m] = (keep[block].astype(f32) + arrived[block].astype(f32)).astype(bf16)
            for bit in bits[::-1]:
                for m in sorted(held):
                    if m & bit:
                        came = swap(held.pop(m), bit).astype(f32)
                        held[m ^ bit] = (held[m ^ bit].astype(f32) + came).astype(bf16)
            sides.append(held[0])
        width = total_cols // n_head
        per_side = n_head // 2
        total = sides[0][:, :width].astype(f32)
        for s in range(1, n_head):
            at = s % per_side
            piece = sides[s // per_side][:, at * width : (at + 1) * width]
            total = total + shift(piece, n_head - s).astype(f32)
        return total

    def sum_everywhere(values_in):
        for bit in [1 << b for b in range(n_dp.bit_length() - 1)]:
            values_in = values_in + swap(values_in, bit)
        for bit in [1 << b for b in range(n_head.bit_length() - 1)]:
            values_in = values_in + swap_head(values_in, bit)
        return values_in

    def per_device(
        latents,
        media_tokens,
        image_counts,
        time_table,
        media_gain,
        media_bias,
        latent_gain,
        latent_bias,
        feed_gain,
        feed_bias,
        query_weight,
        key_weight,
        value_weight,
        out_weight,
        up_weight,
        down_weight,
        cotangent,
    ):
        me = lax.axis_index("dp")
        my_head = lax.axis_index("head")
        images_dp = latents.shape[0] // LAT
        images = images_dp // n_head
        lat_rows = images * LAT
        media_rows = images * PATCH
        half_d = D // 2

        attention_shard = jnp.concatenate(
            [query_weight, key_weight, value_weight, out_weight.T], axis=1
        )
        width = query_weight.shape[1]
        inner = width * n_head
        attention_even, attention_odd = gather(attention_shard)

        cot_cols = cotangent.shape[1]
        full_cot = jnp.zeros((lat_rows, D), bf16)
        for s in range(n_head):
            target = (my_head + s) % n_head
            block = lax.dynamic_slice_in_dim(cotangent, target * lat_rows, lat_rows, 0)
            if s:
                block = shift(block, s)
            source = (my_head - s) % n_head
            full_cot = lax.dynamic_update_slice_in_dim(full_cot, block, source * cot_cols, 1)
        grad_out = to_own(full_cot, me)

        up_even, up_odd = gather(up_weight)
        down_even, down_odd = gather(down_weight.T)

        first_image = me * images_dp + my_head * images
        counts_sum = jnp.cumsum(image_counts)
        starts = counts_sum - image_counts
        image_index = first_image + jnp.arange(images, dtype=jnp.int32)
        latest = jnp.max(
            jnp.where(starts[None, :] <= image_index[:, None], starts[None, :], 0), axis=1
        )
        media_slots = image_index - latest
        slot_match = media_slots[:, None] == jnp.arange(MAX_MEDIA, dtype=jnp.int32)[None, :]
        vectors = jnp.stack(
            [media_gain, media_bias, latent_gain, latent_bias, feed_gain, feed_bias]
        )
        vectors = to_own(vectors, me)
        media_g, media_b, latent_g, latent_b, feed_g, feed_b = [vectors[j : j + 1] for j in range(6)]
        per_image = jnp.dot(
            slot_match.astype(bf16), to_own(time_table, me), preferred_element_type=f32
        )
        media_own = to_own(
            lax.dynamic_slice_in_dim(media_tokens, my_head * media_rows, media_rows, 0), me
        )
        latents_own = to_own(
            lax.dynamic_slice_in_dim(latents, my_head * lat_rows, lat_rows, 0), me
        ).astype(f32)

        media_sum = (
            media_own.reshape(images, PATCH, D).astype(f32) + per_image[:, None, :]
        ).reshape(media_rows, D)
        media_scaled, media_inverse = norm_stats(media_sum)
        media_norm = (media_scaled * media_g + media_b).astype(bf16)
        latent_scaled, latent_inverse = norm_stats(latents_own)
        latent_norm = (latent_scaled * latent_g + latent_b).astype(bf16)

        def column_part(block, at):
            split = block.reshape(block.shape[0], n_head, 4, width)
            return split[:, :, at].reshape(block.shape[0], inner)

        attention_full = jnp.concatenate([attention_even, attention_odd], axis=0)
        query_full, key_full, value_full, out_full = [
            column_part(attention_full, at) for at in range(4)
        ]
        kv_full = jnp.concatenate([key_full, value_full], axis=1)

        query = mm(latent_norm, query_full).astype(bf16)
        media_kv = mm(media_norm, kv_full).astype(bf16)
        latent_kv = mm(latent_norm, kv_full).astype(bf16)
        mixed = attend(query, media_kv, latent_kv)
        hidden = latents_own + mm_nt(mixed, out_full)
        feed_scaled, feed_inverse = norm_stats(hidden)
        feed_norm = (feed_scaled * feed_g + feed_b).astype(bf16)

        up_full = jnp.concatenate([up_even, up_odd], axis=0)
        down_full = jnp.concatenate([down_even, down_odd], axis=0)
        up_proj = mm(feed_norm, up_full)
        activation = gelu_exact(up_proj).astype(bf16)
        result = hidden + mm_nt(activation, down_full)

        plain_out = to_plain(result.astype(bf16), me)
        out_cols = D // n_head
        latents_out = jnp.zeros((images_dp * LAT, out_cols), f32)
        for s in range(n_head):
            target = (my_head + s) % n_head
            block = lax.dynamic_slice_in_dim(plain_out, target * out_cols, out_cols, 1)
            if s:
                block = shift(block, s)
            source = (my_head - s) % n_head
            latents_out = lax.dynamic_update_slice_in_dim(
                latents_out, block.astype(f32), source * lat_rows, 0
            )

        d_act = mm(grad_out, down_full)
        d_up = (d_act * gelu_slope(up_proj)).astype(bf16)
        down_grad = scatter(
            mm_tn(grad_out[:, :half_d], activation).astype(bf16),
            mm_tn(grad_out[:, half_d:], activation).astype(bf16),
        )
        up_grad = scatter(
            mm_tn(feed_norm[:, :half_d], d_up).astype(bf16),
            mm_tn(feed_norm[:, half_d:], d_up).astype(bf16),
        )
        d_feed = mm_nt(d_up, up_full)
        feed_gain_part = jnp.sum(d_feed * feed_scaled, axis=0)
        feed_bias_part = jnp.sum(d_feed, axis=0)
        d_hidden = grad_out.astype(f32) + norm_back(d_feed, feed_scaled, feed_inverse, feed_g)
        d_attention = d_hidden.astype(bf16)
        d_mixed = mm(d_attention, out_full).astype(bf16)

        d_query, d_key_m, d_key_l, d_value_m, d_value_l = attend_back(
            query, media_kv, latent_kv, d_mixed
        )
        d_media_kv = jnp.concatenate([d_key_m, d_value_m], axis=1)
        d_latent_kv = jnp.concatenate([d_key_l, d_value_l], axis=1)
        d_latent_norm = mm_nt(d_query, query_full) + mm_nt(d_latent_kv, kv_full)
        latent_gain_part = jnp.sum(d_latent_norm * latent_scaled, axis=0)
        latent_bias_part = jnp.sum(d_latent_norm, axis=0)
        latent_back = d_hidden + norm_back(d_latent_norm, latent_scaled, latent_inverse, latent_g)

        own_grad = to_plain(latent_back.astype(bf16), me)
        latents_grad = jnp.zeros((images_dp * LAT, D), f32)
        rising, falling = own_grad, own_grad
        latents_grad = lax.dynamic_update_slice_in_dim(
            latents_grad, own_grad.astype(f32), my_head * lat_rows, 0
        )
        for s in range(1, n_head):
            rising = lax.ppermute(rising, "head", [(j, j + 1) for j in range(n_head - 1)])
            falling = lax.ppermute(falling, "head", [(j, j - 1) for j in range(1, n_head)])
            below = jnp.maximum(my_head - s, 0)
            above = jnp.minimum(my_head + s, n_head - 1)
            kept = lax.dynamic_slice_in_dim(latents_grad, below * lat_rows, lat_rows, 0)
            latents_grad = lax.dynamic_update_slice_in_dim(
                latents_grad,
                jnp.where(my_head >= s, rising.astype(f32), kept),
                below * lat_rows,
                0,
            )
            kept = lax.dynamic_slice_in_dim(latents_grad, above * lat_rows, lat_rows, 0)
            latents_grad = lax.dynamic_update_slice_in_dim(
                latents_grad,
                jnp.where(my_head + s < n_head, falling.astype(f32), kept),
                above * lat_rows,
                0,
            )

        def attention_grads(cols):
            wide = mm_tn(media_norm[:, cols], d_media_kv) + mm_tn(latent_norm[:, cols], d_latent_kv)
            query_part = mm_tn(latent_norm[:, cols], d_query)
            out_part = mm_tn(d_attention[:, cols], mixed)
            parts = [query_part, wide[:, :inner], wide[:, inner:], out_part]
            split = [p.astype(bf16).reshape(half_d, n_head, 1, width) for p in parts]
            return jnp.concatenate(split, axis=2).reshape(half_d, 4 * inner)

        attention_grad = scatter(
            attention_grads(slice(0, half_d)), attention_grads(slice(half_d, D))
        )
        query_grad, key_grad, value_grad, out_grad = [
            attention_grad[:, at * width : (at + 1) * width] for at in range(4)
        ]

        d_media_norm = mm_nt(d_media_kv, kv_full)
        media_gain_part = jnp.sum(d_media_norm * media_scaled, axis=0)
        media_bias_part = jnp.sum(d_media_norm, axis=0)
        media_back = norm_back(d_media_norm, media_scaled, media_inverse, media_g)
        image_sums = jnp.sum(media_back.reshape(images, PATCH, D), axis=1)
        time_part = jnp.dot(slot_match.astype(f32).T, image_sums, precision=highest)
        small = jnp.concatenate(
            [
                time_part,
                jnp.stack(
                    [
                        media_gain_part,
                        media_bias_part,
                        latent_gain_part,
                        latent_bias_part,
                        feed_gain_part,
                        feed_bias_part,
                    ]
                ),
            ],
            axis=0,
        )
        small = sum_everywhere(to_plain(small, me))
        return (
            latents_out,
            latents_grad,
            small[:MAX_MEDIA],
            small[MAX_MEDIA],
            small[MAX_MEDIA + 1],
            small[MAX_MEDIA + 2],
            small[MAX_MEDIA + 3],
            small[MAX_MEDIA + 4],
            small[MAX_MEDIA + 5],
            query_grad,
            key_grad,
            value_grad,
            out_grad.T,
            up_grad,
            down_grad.T,
        )

    return per_device


def solution(mesh):
    per_device = make_step(mesh.shape["dp"], mesh.shape["head"])
    rows, both, flipped, whole = P("dp", None), P("dp", "head"), P("head", "dp"), P()
    return jax.shard_map(
        per_device,
        mesh=mesh,
        in_specs=(rows, rows)
        + (whole,) * 8
        + (both, both, both, flipped, both, flipped, both),
        out_specs=(both, rows) + (whole,) * 7 + (both, both, both, flipped, both, flipped),
        check_vma=False,
    )
```

```python
import math

import jax
import jax.numpy as jnp
from jax import lax
from jax.experimental import pallas as pl
from jax.experimental.pallas import tpu as pltpu
from jax.sharding import PartitionSpec as P

D = 1024
DH = 64
LAT = 64
PATCH = 256
MAX_MEDIA = 5
GROUP = 4

epsilon = 1e-05
highest = lax.Precision.HIGHEST
bf16 = jnp.bfloat16
f32 = jnp.float32


def mm(left, right):
    return lax.dot_general(left, right, (((1,), (0,)), ((), ())), preferred_element_type=f32)


def mm_tn(left, right):
    return lax.dot_general(left, right, (((0,), (0,)), ((), ())), preferred_element_type=f32)


def mm_nt(left, right):
    return lax.dot_general(left, right, (((1,), (1,)), ((), ())), preferred_element_type=f32)


def norm_stats(values_in):
    centre = jnp.mean(values_in, axis=-1, keepdims=True)
    shifted = values_in - centre
    spread = jnp.mean(shifted * shifted, axis=-1, keepdims=True)
    inverse = lax.rsqrt(spread + epsilon)
    return (shifted * inverse, inverse)


def norm_back(grad_in, scaled, inverse, norm_gain):
    weighted = grad_in * norm_gain
    return inverse * (
        weighted
        - jnp.mean(weighted, axis=-1, keepdims=True)
        - scaled * jnp.mean(weighted * scaled, axis=-1, keepdims=True)
    )


def gelu_exact(up_proj):
    return up_proj * 0.5 * (1.0 + lax.erf(up_proj * 0.5**0.5))


def gelu_slope(up_proj):
    normal_cdf = 0.5 * (1.0 + lax.erf(up_proj * 0.5**0.5))
    normal_pdf = jnp.exp(-0.5 * up_proj * up_proj) * (2.0 * math.pi) ** (-0.5)
    return normal_cdf + up_proj * normal_pdf


def own_blocks():
    width = GROUP * DH
    rows = lax.broadcasted_iota(jnp.int32, (GROUP * LAT, width), 0) // LAT
    cols = lax.broadcasted_iota(jnp.int32, (GROUP * LAT, width), 1) // DH
    return rows == cols


def spread_heads(block, mask):
    return jnp.where(mask, jnp.concatenate([block] * GROUP, axis=0), jnp.zeros((), block.dtype))


def gather_heads(blocks, mask):
    kept = jnp.where(mask, blocks, 0.0)
    return sum(kept[g * LAT : (g + 1) * LAT] for g in range(GROUP))


def soft_of(query_diag, keys):
    scores = mm_nt(query_diag, keys) * (DH**-0.5)
    expd = jnp.exp(scores - jnp.max(scores, axis=-1, keepdims=True))
    return expd / jnp.sum(expd, axis=-1, keepdims=True)


def attend_kernel(q_ref, km_ref, kl_ref, vm_ref, vl_ref, mixed_ref):
    mask = own_blocks()
    width = GROUP * DH
    for g in range(q_ref.shape[1] // width):
        cols = slice(g * width, (g + 1) * width)
        keys = jnp.concatenate([km_ref[:, cols], kl_ref[:, cols]], axis=0)
        values = jnp.concatenate([vm_ref[:, cols], vl_ref[:, cols]], axis=0)
        soft = soft_of(spread_heads(q_ref[:, cols], mask), keys)
        mixed_ref[:, cols] = gather_heads(mm(soft.astype(bf16), values), mask).astype(bf16)


def attend_back_kernel(
    q_ref, km_ref, kl_ref, vm_ref, vl_ref, dm_ref, dq_ref, dkvm_ref, dkvl_ref
):
    mask = own_blocks()
    width = GROUP * DH
    inner = q_ref.shape[1]
    for g in range(q_ref.shape[1] // width):
        cols = slice(g * width, (g + 1) * width)
        keys = jnp.concatenate([km_ref[:, cols], kl_ref[:, cols]], axis=0)
        values = jnp.concatenate([vm_ref[:, cols], vl_ref[:, cols]], axis=0)
        query_diag = spread_heads(q_ref[:, cols], mask)
        mixed_diag = spread_heads(dm_ref[:, cols], mask)
        soft = soft_of(query_diag, keys)
        d_prob = mm_nt(mixed_diag, values)
        d_value = mm_tn(soft.astype(bf16), mixed_diag).astype(bf16)
        delta = jnp.sum(soft * d_prob, axis=-1, keepdims=True)
        d_scores = (soft * (d_prob - delta)).astype(bf16)
        d_query = gather_heads(mm(d_scores, keys), mask) * (DH**-0.5)
        d_key = (mm_tn(d_scores, query_diag) * (DH**-0.5)).astype(bf16)
        dq_ref[:, cols] = d_query.astype(bf16)
        value_cols = slice(inner + g * width, inner + (g + 1) * width)
        dkvm_ref[:, cols] = d_key[:PATCH]
        dkvl_ref[:, cols] = d_key[PATCH:]
        dkvm_ref[:, value_cols] = d_value[:PATCH]
        dkvl_ref[:, value_cols] = d_value[PATCH:]


def image_spec(rows, cols, block_col=0):
    return pl.BlockSpec((rows, cols), lambda n: (n, block_col))


def attend(query, media_kv, latent_kv):
    inner = query.shape[1]
    images = query.shape[0] // LAT
    return pl.pallas_call(
        attend_kernel,
        grid=(images,),
        in_specs=[
            image_spec(LAT, inner),
            image_spec(PATCH, inner, 0),
            image_spec(LAT, inner, 0),
            image_spec(PATCH, inner, 1),
            image_spec(LAT, inner, 1),
        ],
        out_specs=image_spec(LAT, inner),
        out_shape=jax.ShapeDtypeStruct(query.shape, bf16),
        name="attend",
    )(query, media_kv, latent_kv, media_kv, latent_kv)


def attend_back(query, media_kv, latent_kv, d_mixed):
    inner = query.shape[1]
    images = query.shape[0] // LAT
    return pl.pallas_call(
        attend_back_kernel,
        grid=(images,),
        in_specs=[
            image_spec(LAT, inner),
            image_spec(PATCH, inner, 0),
            image_spec(LAT, inner, 0),
            image_spec(PATCH, inner, 1),
            image_spec(LAT, inner, 1),
            image_spec(LAT, inner),
        ],
        out_specs=[
            image_spec(LAT, inner),
            image_spec(PATCH, 2 * inner),
            image_spec(LAT, 2 * inner),
        ],
        out_shape=[
            jax.ShapeDtypeStruct(shape, bf16)
            for shape in (query.shape, media_kv.shape, latent_kv.shape)
        ],
        name="attend_back",
    )(query, media_kv, latent_kv, media_kv, latent_kv, d_mixed)


UNITS = 512


def hidden_kernel(norm_ref, grad_ref, up_ref, down_ref, act_ref, d_up_ref):
    up_proj = mm(norm_ref[...], up_ref[...])
    d_act = mm(grad_ref[...], down_ref[...])
    act_ref[...] = gelu_exact(up_proj).astype(bf16)
    d_up_ref[...] = (d_act * gelu_slope(up_proj)).astype(bf16)


def hidden_units(feed_norm, grad_out, weights):
    rows = feed_norm.shape[0]
    per_head = weights.shape[1] // 2 // UNITS
    n_head = weights.shape[0] // D
    units = weights.shape[1] // 2 * n_head
    whole = pl.BlockSpec((rows, D), lambda n: (0, 0))
    cols = pl.BlockSpec((rows, UNITS), lambda n: (0, n))
    shape = jax.ShapeDtypeStruct((rows, units), bf16)
    return pl.pallas_call(
        hidden_kernel,
        grid=(units // UNITS,),
        in_specs=[
            whole,
            whole,
            pl.BlockSpec((D, UNITS), lambda n: (n // per_head, n % per_head)),
            pl.BlockSpec((D, UNITS), lambda n: (n // per_head, per_head + n % per_head)),
        ],
        out_specs=[cols, cols],
        out_shape=[shape, shape],
        cost_estimate=pl.CostEstimate(
            flops=4 * rows * D * units, bytes_accessed=4 * D * units, transcendentals=rows * units
        ),
        name="hidden_units",
    )(feed_norm, grad_out, weights, weights)


def features_kernel(hidden_ref, weight_ref, out_ref):
    @pl.when(pl.program_id(0) == 0)
    def _():
        out_ref[...] = jnp.zeros_like(out_ref)

    out_ref[...] += mm_nt(hidden_ref[...], weight_ref[...])


def to_features(units_in, weights, side):
    rows, units = units_in.shape
    per_head = weights.shape[1] // 2 // UNITS
    return pl.pallas_call(
        features_kernel,
        grid=(units // UNITS,),
        in_specs=[
            pl.BlockSpec((rows, UNITS), lambda n: (0, n)),
            pl.BlockSpec(
                (D, UNITS), lambda n: (n // per_head, side * per_head + n % per_head)
            ),
        ],
        out_specs=pl.BlockSpec((rows, D), lambda n: (0, 0)),
        out_shape=jax.ShapeDtypeStruct((rows, D), f32),
        cost_estimate=pl.CostEstimate(
            flops=2 * rows * D * units, bytes_accessed=2 * D * units, transcendentals=0
        ),
        name="to_features",
    )(units_in, weights)


def join(refs):
    return jnp.concatenate([ref[...] for ref in refs], axis=1)


def unit_grad_kernel(place_ref, *refs):
    left, (right_ref, out_ref) = refs[:-2], refs[-2:]
    out_ref[...] = mm_tn(join(left), right_ref[...]).astype(bf16)


def attention_grad_kernel(place_ref, *refs):
    count = (len(refs) - 7) // 3
    latent, media, attention = refs[:count], refs[count : 2 * count], refs[2 * count : 3 * count]
    dq_ref, dkm_ref, dvm_ref, dkl_ref, dvl_ref, mixed_ref, out_ref = refs[3 * count :]
    latent_rows, media_rows = join(latent), join(media)
    query_part = mm_tn(latent_rows, dq_ref[...])
    kv_part = mm_tn(media_rows, join((dkm_ref, dvm_ref))) + mm_tn(
        latent_rows, join((dkl_ref, dvl_ref))
    )
    out_part = mm_tn(join(attention), mixed_ref[...])
    out_ref[...] = jnp.concatenate([query_part, kv_part, out_part], axis=1).astype(bf16)


def make_step(n_dp, n_head):
    def swap(block, bit):
        return lax.ppermute(block, "dp", [(j, j ^ bit) for j in range(n_dp)])

    def shift(block, step):
        return lax.ppermute(block, "head", [(j, (j + step) % n_head) for j in range(n_head)])

    def swap_head(block, bit):
        return lax.ppermute(block, "head", [(j, j ^ bit) for j in range(n_head)])

    ordered = [1 << b for b in range(1, n_dp.bit_length() - 1)]
    paths = (ordered, ordered[::-1])
    evens = list(range(0, n_dp, 2))
    places = evens + [m | 1 for m in evens]
    size = D // n_dp
    wide = size % 128 == 0
    half_blocks = D // 2 // max(size, 128)

    def left_blocks(values_in, me, half):
        rows = values_in.shape[0]
        if wide:
            specs = [
                pl.BlockSpec((rows, size), lambda n, at, m=m: (0, at[0] ^ m))
                for m in places[half * half_blocks : (half + 1) * half_blocks]
            ]
        else:
            parts = [lax.dynamic_slice_in_dim(values_in, (me ^ m) * size, size, 1) for m in places]
            values_in = jnp.concatenate(parts, axis=1)
            specs = [
                pl.BlockSpec((rows, 128), lambda n, at, b=b: (0, b))
                for b in range(half * half_blocks, (half + 1) * half_blocks)
            ]
        return ([values_in] * half_blocks, specs)

    def unit_grad(left, right, here, half):
        rows, units = right.shape
        per_head = units // n_head // UNITS
        operands, specs = left_blocks(left, here[0], half)
        return pl.pallas_call(
            unit_grad_kernel,
            grid_spec=pltpu.PrefetchScalarGridSpec(
                num_scalar_prefetch=1,
                grid=(units // UNITS,),
                in_specs=specs
                + [
                    pl.BlockSpec(
                        (rows, UNITS),
                        lambda n, at: (
                            0,
                            lax.rem(at[1] + n_head - n // per_head, n_head) * per_head
                            + n % per_head,
                        ),
                    )
                ],
                out_specs=pl.BlockSpec((D // 2, UNITS), lambda n, at: (0, n)),
            ),
            out_shape=jax.ShapeDtypeStruct((D // 2, units), bf16),
            cost_estimate=pl.CostEstimate(
                flops=rows * D * units, bytes_accessed=D * units, transcendentals=0
            ),
            name="unit_grad",
        )(here, *operands, right)

    def attention_grad(
        latent_norm, media_norm, d_attention, d_query, d_media_kv, d_latent_kv, mixed, here, half
    ):
        inner = d_query.shape[1]
        width = inner // n_head
        operands, specs = [], []
        for left in (latent_norm, media_norm, d_attention):
            more, more_specs = left_blocks(left, here[0], half)
            operands, specs = operands + more, specs + more_specs

        def group(rows, start):
            return pl.BlockSpec(
                (rows, width), lambda n, at: (0, start + lax.rem(at[1] + n_head - n, n_head))
            )

        lat_rows, media_rows = d_query.shape[0], d_media_kv.shape[0]
        return pl.pallas_call(
            attention_grad_kernel,
            grid_spec=pltpu.PrefetchScalarGridSpec(
                num_scalar_prefetch=1,
                grid=(n_head,),
                in_specs=specs
                + [
                    group(lat_rows, 0),
                    group(media_rows, 0),
                    group(media_rows, n_head),
                    group(lat_rows, 0),
                    group(lat_rows, n_head),
                    group(lat_rows, 0),
                ],
                out_specs=pl.BlockSpec((D // 2, 4 * width), lambda n, at: (0, n)),
            ),
            out_shape=jax.ShapeDtypeStruct((D // 2, 4 * inner), bf16),
            cost_estimate=pl.CostEstimate(
                flops=2 * D * inner * (media_rows + 2 * lat_rows),
                bytes_accessed=4 * D * inner,
                transcendentals=0,
            ),
            name="attention_grad",
        )(here, *operands, d_query, d_media_kv, d_media_kv, d_latent_kv, d_latent_kv, mixed)


    def gather(shard):
        columns = [shard] + [shift(shard, s) for s in range(1, n_head)]
        half = n_head // 2
        pieces = {}
        for side, bits in enumerate(paths):
            held = {0: jnp.concatenate(columns[side * half : (side + 1) * half], axis=1)}
            for bit in bits:
                for m in list(held):
                    held[m | bit] = swap(held[m], bit)
            for m in evens:
                pieces[m, side] = held[m]
                pieces[m | 1, side] = swap(held[m], 1)
        return pieces

    def assemble(pieces, here):
        keys = sorted(pieces)
        rows, cols = pieces[keys[0]].shape
        width = cols // (n_head // 2) // 4
        inner = width * n_head

        def kernel(place_ref, *refs):
            sources, (query_ref, kv_ref, out_ref) = refs[:-3], refs[-3:]
            for (m, side), ref in zip(keys, sources):
                at = pl.ds(pl.multiple_of((place_ref[0] ^ m) * rows, rows), rows)
                for k in range(n_head // 2):
                    s = side * (n_head // 2) + k
                    head = lax.rem(place_ref[1] + n_head - s, n_head)
                    base = k * 4 * width
                    to = pl.ds(pl.multiple_of(head * width, width), width)
                    to_value = pl.ds(pl.multiple_of(inner + head * width, width), width)
                    query_ref[at, to] = ref[:, base : base + width]
                    kv_ref[at, to] = ref[:, base + width : base + 2 * width]
                    kv_ref[at, to_value] = ref[:, base + 2 * width : base + 3 * width]
                    out_ref[at, to] = ref[:, base + 3 * width : base + 4 * width]

        return pl.pallas_call(
            kernel,
            grid_spec=pltpu.PrefetchScalarGridSpec(
                num_scalar_prefetch=1,
                grid=(1,),
                in_specs=[pl.BlockSpec((rows, cols), lambda n, at: (0, 0)) for _ in keys],
                out_specs=[
                    pl.BlockSpec((D, inner), lambda n, at: (0, 0)),
                    pl.BlockSpec((D, 2 * inner), lambda n, at: (0, 0)),
                    pl.BlockSpec((D, inner), lambda n, at: (0, 0)),
                ],
            ),
            out_shape=[jax.ShapeDtypeStruct((D, c), bf16) for c in (inner, 2 * inner, inner)],
            name="assemble",
        )(here, *[pieces[key] for key in keys])

    def scatter(keep, send):
        arrived = swap(send, 1)
        total_rows, total_cols = keep.shape
        rows = total_rows // len(evens)
        half = total_cols // 2
        sides = []
        for bits, side in zip(paths, (0, 1)):
            cols = slice(side * half, (side + 1) * half)
            held = keep[:, cols].astype(f32) + arrived[:, cols].astype(f32)
            order = evens
            for bit in bits[::-1]:
                away = [order.index(m) for m in order if m & bit]
                stay = [order.index(m) for m in order if not m & bit]
                pick = lambda which: jnp.concatenate(
                    [held[at * rows : (at + 1) * rows] for at in which], axis=0
                )
                came = swap(pick(away).astype(bf16), bit)
                held = pick(stay) + came.astype(f32)
                order = [order[at] for at in stay]
            sides.append(held.astype(bf16))
        width = total_cols // n_head
        per_side = n_head // 2
        total = sides[0][:, :width].astype(f32)
        for s in range(1, n_head):
            at = s % per_side
            piece = sides[s // per_side][:, at * width : (at + 1) * width]
            total = total + shift(piece, n_head - s).astype(f32)
        return total

    def sum_everywhere(values_in):
        for bit in [1 << b for b in range(n_dp.bit_length() - 1)]:
            values_in = values_in + swap(values_in, bit)
        for bit in [1 << b for b in range(n_head.bit_length() - 1)]:
            values_in = values_in + swap_head(values_in, bit)
        return values_in

    def share_rows(own, here):
        rows = own.shape[0]
        below, above = [own], [own]
        for _ in range(1, n_head):
            below.append(
                lax.ppermute(below[-1], "head", [(j, j + 1) for j in range(n_head - 1)])
            )
            above.append(lax.ppermute(above[-1], "head", [(j, j - 1) for j in range(1, n_head)]))

        def kernel(place_ref, own_ref, *refs):
            lower, upper, out_ref = refs[: n_head - 1], refs[n_head - 1 : -1], refs[-1]
            away = pl.program_id(0) - place_ref[1]

            @pl.when(away == 0)
            def _():
                out_ref[...] = own_ref[...].astype(f32)

            for s in range(1, n_head):

                @pl.when(away == -s)
                def _(s=s):
                    out_ref[...] = lower[s - 1][...].astype(f32)

                @pl.when(away == s)
                def _(s=s):
                    out_ref[...] = upper[s - 1][...].astype(f32)

        one = pl.BlockSpec((rows, D), lambda n, at: (0, 0))
        return pl.pallas_call(
            kernel,
            grid_spec=pltpu.PrefetchScalarGridSpec(
                num_scalar_prefetch=1,
                grid=(n_head,),
                in_specs=[one] * (2 * n_head - 1),
                out_specs=pl.BlockSpec((rows, D), lambda n, at: (n, 0)),
            ),
            out_shape=jax.ShapeDtypeStruct((n_head * rows, D), f32),
            name="share_rows",
        )(here, own, *below[1:], *above[1:])

    def per_device(
        latents,
        media_tokens,
        image_counts,
        time_table,
        media_gain,
        media_bias,
        latent_gain,
        latent_bias,
        feed_gain,
        feed_bias,
        query_weight,
        key_weight,
        value_weight,
        out_weight,
        up_weight,
        down_weight,
        cotangent,
    ):
        me = lax.axis_index("dp")
        my_head = lax.axis_index("head")
        here = jnp.stack([me, my_head]).astype(jnp.int32)
        images_dp = latents.shape[0] // LAT
        images = images_dp // n_head
        lat_rows = images * LAT
        media_rows = images * PATCH

        pieces = gather(
            jnp.concatenate([query_weight, key_weight, value_weight, out_weight.T], axis=1)
        )
        unit_weights = lax.all_gather(
            jnp.concatenate([up_weight, down_weight.T], axis=1), ("head", "dp"), axis=0, tiled=True
        )
        query_full, kv_full, out_full = assemble(pieces, here)

        cot_cols = cotangent.shape[1]
        grad_out = jnp.zeros((lat_rows, D), bf16)
        for s in range(n_head):
            target = (my_head + s) % n_head
            block = lax.dynamic_slice_in_dim(cotangent, target * lat_rows, lat_rows, 0)
            if s:
                block = shift(block, s)
            source = (my_head - s) % n_head
            grad_out = lax.dynamic_update_slice_in_dim(grad_out, block, source * cot_cols, 1)

        first_image = me * images_dp + my_head * images
        counts_sum = jnp.cumsum(image_counts)
        starts = counts_sum - image_counts
        image_index = first_image + jnp.arange(images, dtype=jnp.int32)
        latest = jnp.max(
            jnp.where(starts[None, :] <= image_index[:, None], starts[None, :], 0), axis=1
        )
        media_slots = image_index - latest
        slot_match = media_slots[:, None] == jnp.arange(MAX_MEDIA, dtype=jnp.int32)[None, :]
        per_image = jnp.dot(slot_match.astype(bf16), time_table, preferred_element_type=f32)
        media_own = lax.dynamic_slice_in_dim(media_tokens, my_head * media_rows, media_rows, 0)
        latents_own = lax.dynamic_slice_in_dim(latents, my_head * lat_rows, lat_rows, 0)
        latents_own = latents_own.astype(f32)

        media_sum = (
            media_own.reshape(images, PATCH, D).astype(f32) + per_image[:, None, :]
        ).reshape(media_rows, D)
        media_scaled, media_inverse = norm_stats(media_sum)
        media_norm = (media_scaled * media_gain + media_bias).astype(bf16)
        latent_scaled, latent_inverse = norm_stats(latents_own)
        latent_norm = (latent_scaled * latent_gain + latent_bias).astype(bf16)

        query = mm(latent_norm, query_full).astype(bf16)
        media_kv = mm(media_norm, kv_full).astype(bf16)
        latent_kv = mm(latent_norm, kv_full).astype(bf16)
        mixed = attend(query, media_kv, latent_kv)
        hidden = latents_own + mm_nt(mixed, out_full)
        feed_scaled, feed_inverse = norm_stats(hidden)
        feed_norm = (feed_scaled * feed_gain + feed_bias).astype(bf16)

        activation, d_up = hidden_units(feed_norm, grad_out, unit_weights)
        down_grad = scatter(
            unit_grad(grad_out, activation, here, 0), unit_grad(grad_out, activation, here, 1)
        )
        up_grad = scatter(unit_grad(feed_norm, d_up, here, 0), unit_grad(feed_norm, d_up, here, 1))
        d_feed = to_features(d_up, unit_weights, 0)
        feed_gain_part = jnp.sum(d_feed * feed_scaled, axis=0)
        feed_bias_part = jnp.sum(d_feed, axis=0)
        d_hidden = grad_out.astype(f32) + norm_back(d_feed, feed_scaled, feed_inverse, feed_gain)
        d_attention = d_hidden.astype(bf16)
        d_mixed = mm(d_attention, out_full).astype(bf16)

        d_query, d_media_kv, d_latent_kv = attend_back(query, media_kv, latent_kv, d_mixed)
        d_latent_norm = mm_nt(d_query, query_full) + mm_nt(d_latent_kv, kv_full)
        latent_gain_part = jnp.sum(d_latent_norm * latent_scaled, axis=0)
        latent_bias_part = jnp.sum(d_latent_norm, axis=0)
        latent_back = d_hidden + norm_back(
            d_latent_norm, latent_scaled, latent_inverse, latent_gain
        )
        latents_grad = share_rows(latent_back.astype(bf16), here)

        keep, send = [
            attention_grad(
                latent_norm,
                media_norm,
                d_attention,
                d_query,
                d_media_kv,
                d_latent_kv,
                mixed,
                here,
                half,
            )
            for half in (0, 1)
        ]
        attention_grads = scatter(keep, send)
        width = query_weight.shape[1]
        query_grad, key_grad, value_grad, out_grad = [
            attention_grads[:, at * width : (at + 1) * width] for at in range(4)
        ]

        d_media_norm = mm_nt(d_media_kv, kv_full)
        media_gain_part = jnp.sum(d_media_norm * media_scaled, axis=0)
        media_bias_part = jnp.sum(d_media_norm, axis=0)
        media_back = norm_back(d_media_norm, media_scaled, media_inverse, media_gain)
        image_sums = jnp.sum(media_back.reshape(images, PATCH, D), axis=1)
        time_part = jnp.dot(slot_match.astype(f32).T, image_sums, precision=highest)
        small = jnp.concatenate(
            [
                time_part,
                jnp.stack(
                    [
                        media_gain_part,
                        media_bias_part,
                        latent_gain_part,
                        latent_bias_part,
                        feed_gain_part,
                        feed_bias_part,
                    ]
                ),
            ],
            axis=0,
        )
        small = sum_everywhere(small)

        result = (hidden + to_features(activation, unit_weights, 1)).astype(bf16)
        out_cols = D // n_head
        latents_out = jnp.zeros((images_dp * LAT, out_cols), f32)
        for s in range(n_head):
            target = (my_head + s) % n_head
            block = lax.dynamic_slice_in_dim(result, target * out_cols, out_cols, 1)
            if s:
                block = shift(block, s)
            source = (my_head - s) % n_head
            latents_out = lax.dynamic_update_slice_in_dim(
                latents_out, block.astype(f32), source * lat_rows, 0
            )
        return (
            latents_out,
            latents_grad,
            small[:MAX_MEDIA],
            small[MAX_MEDIA],
            small[MAX_MEDIA + 1],
            small[MAX_MEDIA + 2],
            small[MAX_MEDIA + 3],
            small[MAX_MEDIA + 4],
            small[MAX_MEDIA + 5],
            query_grad,
            key_grad,
            value_grad,
            out_grad.T,
            up_grad,
            down_grad.T,
        )

    return per_device


def solution(mesh):
    per_device = make_step(mesh.shape["dp"], mesh.shape["head"])
    rows, both, flipped, whole = P("dp", None), P("dp", "head"), P("head", "dp"), P()
    return jax.shard_map(
        per_device,
        mesh=mesh,
        in_specs=(rows, rows)
        + (whole,) * 8
        + (both, both, both, flipped, both, flipped, both),
        out_specs=(both, rows) + (whole,) * 7 + (both, both, both, flipped, both, flipped),
        check_vma=False,
    )
```

```python
import math

import jax
import jax.numpy as jnp
from jax import lax
from jax.experimental import pallas as pl
from jax.experimental.pallas import tpu as pltpu
from jax.sharding import PartitionSpec as P


D = 1024
DH = 64
LAT = 64
PATCH = 256
MAX_MEDIA = 5
GROUP = 4

epsilon = 1e-05
highest = lax.Precision.HIGHEST
bf16 = jnp.bfloat16
f32 = jnp.float32


def mm(left, right):
    return lax.dot_general(left, right, (((1,), (0,)), ((), ())), preferred_element_type=f32)


def mm_tn(left, right):
    return lax.dot_general(left, right, (((0,), (0,)), ((), ())), preferred_element_type=f32)


def mm_nt(left, right):
    return lax.dot_general(left, right, (((1,), (1,)), ((), ())), preferred_element_type=f32)


def norm_stats(values_in):
    centre = jnp.mean(values_in, axis=-1, keepdims=True)
    shifted = values_in - centre
    spread = jnp.mean(shifted * shifted, axis=-1, keepdims=True)
    inverse = lax.rsqrt(spread + epsilon)
    return (shifted * inverse, inverse)


def norm_back(grad_in, scaled, inverse, norm_gain):
    weighted = grad_in * norm_gain
    return inverse * (
        weighted
        - jnp.mean(weighted, axis=-1, keepdims=True)
        - scaled * jnp.mean(weighted * scaled, axis=-1, keepdims=True)
    )


def gelu_exact(up_proj):
    return up_proj * 0.5 * (1.0 + lax.erf(up_proj * 0.5**0.5))


def gelu_slope(up_proj):
    normal_cdf = 0.5 * (1.0 + lax.erf(up_proj * 0.5**0.5))
    normal_pdf = jnp.exp(-0.5 * up_proj * up_proj) * (2.0 * math.pi) ** (-0.5)
    return normal_cdf + up_proj * normal_pdf


def own_blocks():
    width = GROUP * DH
    rows = lax.broadcasted_iota(jnp.int32, (GROUP * LAT, width), 0) // LAT
    cols = lax.broadcasted_iota(jnp.int32, (GROUP * LAT, width), 1) // DH
    return rows == cols


def spread_heads(block, mask):
    return jnp.where(mask, jnp.concatenate([block] * GROUP, axis=0), jnp.zeros((), block.dtype))


def gather_heads(blocks, mask):
    kept = jnp.where(mask, blocks, 0.0)
    return sum(kept[g * LAT : (g + 1) * LAT] for g in range(GROUP))


def soft_of(query_diag, keys):
    scores = mm_nt(query_diag, keys) * (DH**-0.5)
    expd = jnp.exp(scores - jnp.max(scores, axis=-1, keepdims=True))
    return expd / jnp.sum(expd, axis=-1, keepdims=True)


def attend_kernel(q_ref, km_ref, kl_ref, vm_ref, vl_ref, mixed_ref):
    mask = own_blocks()
    width = GROUP * DH
    for g in range(q_ref.shape[1] // width):
        cols = slice(g * width, (g + 1) * width)
        keys = jnp.concatenate([km_ref[:, cols], kl_ref[:, cols]], axis=0)
        values = jnp.concatenate([vm_ref[:, cols], vl_ref[:, cols]], axis=0)
        soft = soft_of(spread_heads(q_ref[:, cols], mask), keys)
        mixed_ref[:, cols] = gather_heads(mm(soft.astype(bf16), values), mask).astype(bf16)


def attend_back_kernel(
    q_ref, km_ref, kl_ref, vm_ref, vl_ref, dm_ref, dq_ref, dkvm_ref, dkvl_ref
):
    mask = own_blocks()
    width = GROUP * DH
    inner = q_ref.shape[1]
    for g in range(q_ref.shape[1] // width):
        cols = slice(g * width, (g + 1) * width)
        keys = jnp.concatenate([km_ref[:, cols], kl_ref[:, cols]], axis=0)
        values = jnp.concatenate([vm_ref[:, cols], vl_ref[:, cols]], axis=0)
        query_diag = spread_heads(q_ref[:, cols], mask)
        mixed_diag = spread_heads(dm_ref[:, cols], mask)
        soft = soft_of(query_diag, keys)
        d_prob = mm_nt(mixed_diag, values)
        d_value = mm_tn(soft.astype(bf16), mixed_diag).astype(bf16)
        delta = jnp.sum(soft * d_prob, axis=-1, keepdims=True)
        d_scores = (soft * (d_prob - delta)).astype(bf16)
        d_query = gather_heads(mm(d_scores, keys), mask) * (DH**-0.5)
        d_key = (mm_tn(d_scores, query_diag) * (DH**-0.5)).astype(bf16)
        dq_ref[:, cols] = d_query.astype(bf16)
        value_cols = slice(inner + g * width, inner + (g + 1) * width)
        dkvm_ref[:, cols] = d_key[:PATCH]
        dkvl_ref[:, cols] = d_key[PATCH:]
        dkvm_ref[:, value_cols] = d_value[:PATCH]
        dkvl_ref[:, value_cols] = d_value[PATCH:]


def image_spec(rows, cols, block_col=0):
    return pl.BlockSpec((rows, cols), lambda n: (n, block_col))


def attend(query, media_kv, latent_kv):
    inner = query.shape[1]
    images = query.shape[0] // LAT
    return pl.pallas_call(
        attend_kernel,
        grid=(images,),
        in_specs=[
            image_spec(LAT, inner),
            image_spec(PATCH, inner, 0),
            image_spec(LAT, inner, 0),
            image_spec(PATCH, inner, 1),
            image_spec(LAT, inner, 1),
        ],
        out_specs=image_spec(LAT, inner),
        out_shape=jax.ShapeDtypeStruct(query.shape, bf16),
        name="attend",
    )(query, media_kv, latent_kv, media_kv, latent_kv)


def attend_back(query, media_kv, latent_kv, d_mixed):
    inner = query.shape[1]
    images = query.shape[0] // LAT
    return pl.pallas_call(
        attend_back_kernel,
        grid=(images,),
        in_specs=[
            image_spec(LAT, inner),
            image_spec(PATCH, inner, 0),
            image_spec(LAT, inner, 0),
            image_spec(PATCH, inner, 1),
            image_spec(LAT, inner, 1),
            image_spec(LAT, inner),
        ],
        out_specs=[
            image_spec(LAT, inner),
            image_spec(PATCH, 2 * inner),
            image_spec(LAT, 2 * inner),
        ],
        out_shape=[
            jax.ShapeDtypeStruct(shape, bf16)
            for shape in (query.shape, media_kv.shape, latent_kv.shape)
        ],
        name="attend_back",
    )(query, media_kv, latent_kv, media_kv, latent_kv, d_mixed)


EARLY = 256


def unit_specs(main, extra, side):
    return [
        pl.BlockSpec((D, weights.shape[1] // 2), lambda n: (n, side)) for weights in (main, extra)
    ]


def hidden_kernel(norm_ref, grad_ref, up_ref, up_more, down_ref, down_more, act_ref, d_up_ref):
    start = 0
    for up, down in ((up_ref, down_ref), (up_more, down_more)):
        cols = slice(start, start + up.shape[1])
        start += up.shape[1]
        up_proj = mm(norm_ref[...], up[...])
        d_act = mm(grad_ref[...], down[...])
        act_ref[:, cols] = gelu_exact(up_proj).astype(bf16)
        d_up_ref[:, cols] = (d_act * gelu_slope(up_proj)).astype(bf16)


def hidden_units(feed_norm, grad_out, main, extra):
    rows = feed_norm.shape[0]
    n_head = main.shape[0] // D
    per_head = (main.shape[1] + extra.shape[1]) // 2
    units = per_head * n_head
    whole = pl.BlockSpec((rows, D), lambda n: (0, 0))
    cols = pl.BlockSpec((rows, per_head), lambda n: (0, n))
    shape = jax.ShapeDtypeStruct((rows, units), bf16)
    return pl.pallas_call(
        hidden_kernel,
        grid=(n_head,),
        in_specs=[whole, whole] + unit_specs(main, extra, 0) + unit_specs(main, extra, 1),
        out_specs=[cols, cols],
        out_shape=[shape, shape],
        cost_estimate=pl.CostEstimate(
            flops=4 * rows * D * units, bytes_accessed=4 * D * units, transcendentals=rows * units
        ),
        name="hidden_units",
    )(feed_norm, grad_out, main, extra, main, extra)


def add_features(units_ref, weight_ref, more_ref, total):
    @pl.when(pl.program_id(0) == 0)
    def _():
        total[...] = jnp.zeros_like(total)

    split = weight_ref.shape[1]
    total[...] += mm_nt(units_ref[:, :split], weight_ref[...])
    total[...] += mm_nt(units_ref[:, split:], more_ref[...])


def feed_out_kernel(units_ref, weight_ref, more_ref, hidden_ref, out_ref, total):
    add_features(units_ref, weight_ref, more_ref, total)

    @pl.when(pl.program_id(0) == pl.num_programs(0) - 1)
    def _():
        out_ref[...] = (hidden_ref[...] + total[...]).astype(bf16)


def d_feed_kernel(
    units_ref,
    weight_ref,
    more_ref,
    hidden_ref,
    grad_ref,
    gain_ref,
    out_weight_ref,
    d_hidden_ref,
    d_attention_ref,
    d_mixed_ref,
    gain_out,
    bias_out,
    total,
):
    add_features(units_ref, weight_ref, more_ref, total)

    @pl.when(pl.program_id(0) == pl.num_programs(0) - 1)
    def _():
        d_feed = total[...]
        scaled, inverse = norm_stats(hidden_ref[...])
        gain_out[...] = jnp.sum(d_feed * scaled, axis=0, keepdims=True)
        bias_out[...] = jnp.sum(d_feed, axis=0, keepdims=True)
        d_hidden = grad_ref[...].astype(f32) + norm_back(d_feed, scaled, inverse, gain_ref[...])
        d_hidden_ref[...] = d_hidden
        d_attention_ref[...] = d_hidden.astype(bf16)
        d_mixed_ref[...] = mm(d_hidden.astype(bf16), out_weight_ref[...]).astype(bf16)


def to_features(kernel, units_in, main, extra, side, others, out_shapes):
    rows, units = units_in.shape
    n_head = main.shape[0] // D
    return pl.pallas_call(
        kernel,
        grid=(n_head,),
        in_specs=[pl.BlockSpec((rows, units // n_head), lambda n: (0, n))]
        + unit_specs(main, extra, side)
        + [pl.BlockSpec(other.shape, lambda n: (0, 0)) for other in others],
        out_specs=[pl.BlockSpec(shape.shape, lambda n: (0, 0)) for shape in out_shapes],
        out_shape=out_shapes,
        scratch_shapes=[pltpu.VMEM((rows, D), f32)],
        cost_estimate=pl.CostEstimate(
            flops=2 * rows * D * units, bytes_accessed=2 * D * units, transcendentals=0
        ),
    )(units_in, main, extra, *others)


def media_back_kernel(
    place_ref, tokens_ref, added_ref, gain_ref, d_kv_ref, weight_ref, gain_out, bias_out, sum_out
):
    @pl.when(pl.program_id(0) == 0)
    def _():
        gain_out[...] = jnp.zeros_like(gain_out)
        bias_out[...] = jnp.zeros_like(bias_out)

    scaled, inverse = norm_stats(tokens_ref[...].astype(f32) + added_ref[0])
    d_norm = mm_nt(d_kv_ref[...], weight_ref[...])
    gain_out[...] += jnp.sum(d_norm * scaled, axis=0, keepdims=True)
    bias_out[...] += jnp.sum(d_norm, axis=0, keepdims=True)
    back = norm_back(d_norm, scaled, inverse, gain_ref[...])
    sum_out[0] = jnp.sum(back, axis=0, keepdims=True)


def media_back(media_tokens, per_image, media_gain, d_media_kv, kv_full, here):
    images = per_image.shape[0]
    row = pl.BlockSpec((1, D), lambda n, at: (0, 0))
    own_row = pl.BlockSpec((1, 1, D), lambda n, at: (n, 0, 0))
    cols = d_media_kv.shape[1]
    gain_sum, bias_sum, sums = pl.pallas_call(
        media_back_kernel,
        grid_spec=pltpu.PrefetchScalarGridSpec(
            num_scalar_prefetch=1,
            grid=(images,),
            in_specs=[
                pl.BlockSpec((PATCH, D), lambda n, at: (at[1] * images + n, 0)),
                own_row,
                row,
                pl.BlockSpec((PATCH, cols), lambda n, at: (n, 0)),
                pl.BlockSpec((D, cols), lambda n, at: (0, 0)),
            ],
            out_specs=[row, row, own_row],
        ),
        out_shape=[
            jax.ShapeDtypeStruct((1, D), f32),
            jax.ShapeDtypeStruct((1, D), f32),
            jax.ShapeDtypeStruct((images, 1, D), f32),
        ],
        cost_estimate=pl.CostEstimate(
            flops=2 * images * PATCH * D * cols,
            bytes_accessed=4 * images * PATCH * D,
            transcendentals=0,
        ),
        name="media_back",
    )(here, media_tokens, per_image[:, None, :], media_gain[None, :], d_media_kv, kv_full)
    return (gain_sum[0], bias_sum[0], sums[:, 0, :])


def join(refs):
    return jnp.concatenate([ref[...] for ref in refs], axis=1)


def unit_grad_kernel(place_ref, *refs):
    left, (right_ref, out_ref) = refs[:-2], refs[-2:]
    out_ref[...] = mm_tn(join(left), right_ref[...]).astype(bf16)


def attention_grad_kernel(place_ref, *refs):
    count = (len(refs) - 7) // 3
    latent, media, attention = refs[:count], refs[count : 2 * count], refs[2 * count : 3 * count]
    dq_ref, dkm_ref, dvm_ref, dkl_ref, dvl_ref, mixed_ref, out_ref = refs[3 * count :]
    latent_rows, media_rows = join(latent), join(media)
    query_part = mm_tn(latent_rows, dq_ref[...])
    kv_part = mm_tn(media_rows, join((dkm_ref, dvm_ref))) + mm_tn(
        latent_rows, join((dkl_ref, dvl_ref))
    )
    out_part = mm_tn(join(attention), mixed_ref[...])
    out_ref[...] = jnp.concatenate([query_part, kv_part, out_part], axis=1).astype(bf16)


def make_step(n_dp, n_head):
    def swap(block, bit):
        return lax.ppermute(block, "dp", [(j, j ^ bit) for j in range(n_dp)])

    def shift(block, step):
        return lax.ppermute(block, "head", [(j, (j + step) % n_head) for j in range(n_head)])

    def swap_head(block, bit):
        return lax.ppermute(block, "head", [(j, j ^ bit) for j in range(n_head)])

    ordered = [1 << b for b in range(1, n_dp.bit_length() - 1)]
    paths = (ordered, ordered[::-1])
    evens = list(range(0, n_dp, 2))
    size = D // n_dp
    wide = size % 128 == 0
    half_blocks = D // 2 // max(size, 128)

    def send_order(bits):
        order = [0]
        for bit in bits:
            order = order + [m | bit for m in order]
        return order

    orders = [send_order(bits) for bits in paths]

    def left_blocks(values_in, me, half, steps):
        rows = values_in.shape[0]
        if wide:
            specs = [
                pl.BlockSpec(
                    (rows, size),
                    lambda n, at, m=m, k=k: (0, at[0] ^ jnp.where(n < steps // 2, m, k)),
                )
                for m, k in zip(*[[m | half for m in order] for order in orders])
            ]
        else:
            parts = [
                lax.dynamic_slice_in_dim(values_in, (me ^ (m | odd)) * size, size, 1)
                for order in orders
                for odd in (0, 1)
                for m in order
            ]
            values_in = jnp.concatenate(parts, axis=1)
            specs = [
                pl.BlockSpec(
                    (rows, 128),
                    lambda n, at, b=b: (0, b + jnp.where(n < steps // 2, 0, D // 128)),
                )
                for b in range(half * half_blocks, (half + 1) * half_blocks)
            ]
        return ([values_in] * half_blocks, specs)

    def unit_grad(left, right, here, half):
        rows, units = right.shape
        block = units // n_head
        operands, specs = left_blocks(left, here[0], half, n_head)
        return pl.pallas_call(
            unit_grad_kernel,
            grid_spec=pltpu.PrefetchScalarGridSpec(
                num_scalar_prefetch=1,
                grid=(n_head,),
                in_specs=specs
                + [
                    pl.BlockSpec(
                        (rows, block), lambda n, at: (0, lax.rem(at[1] + n_head - n, n_head))
                    )
                ],
                out_specs=pl.BlockSpec((D // 2, block), lambda n, at: (0, n)),
            ),
            out_shape=jax.ShapeDtypeStruct((D // 2, units), bf16),
            cost_estimate=pl.CostEstimate(
                flops=rows * D * units, bytes_accessed=D * units, transcendentals=0
            ),
            name="unit_grad",
        )(here, *operands, right)

    def attention_grad(
        latent_norm, media_norm, d_attention, d_query, d_media_kv, d_latent_kv, mixed, here, half
    ):
        inner = d_query.shape[1]
        width = inner // n_head
        operands, specs = [], []
        for left in (latent_norm, media_norm, d_attention):
            more, more_specs = left_blocks(left, here[0], half, n_head)
            operands, specs = operands + more, specs + more_specs

        def group(rows, start):
            return pl.BlockSpec(
                (rows, width), lambda n, at: (0, start + lax.rem(at[1] + n_head - n, n_head))
            )

        lat_rows, media_rows = d_query.shape[0], d_media_kv.shape[0]
        return pl.pallas_call(
            attention_grad_kernel,
            grid_spec=pltpu.PrefetchScalarGridSpec(
                num_scalar_prefetch=1,
                grid=(n_head,),
                in_specs=specs
                + [
                    group(lat_rows, 0),
                    group(media_rows, 0),
                    group(media_rows, n_head),
                    group(lat_rows, 0),
                    group(lat_rows, n_head),
                    group(lat_rows, 0),
                ],
                out_specs=pl.BlockSpec((D // 2, 4 * width), lambda n, at: (0, n)),
            ),
            out_shape=jax.ShapeDtypeStruct((D // 2, 4 * inner), bf16),
            cost_estimate=pl.CostEstimate(
                flops=2 * D * inner * (media_rows + 2 * lat_rows),
                bytes_accessed=4 * D * inner,
                transcendentals=0,
            ),
            name="attention_grad",
        )(here, *operands, d_query, d_media_kv, d_media_kv, d_latent_kv, d_latent_kv, mixed)


    def gather(shard):
        columns = [shard] + [shift(shard, s) for s in range(1, n_head)]
        half = n_head // 2
        pieces = {}
        for side, bits in enumerate(paths):
            held = {0: jnp.concatenate(columns[side * half : (side + 1) * half], axis=1)}
            for bit in bits:
                for m in list(held):
                    held[m | bit] = swap(held[m], bit)
            for m in evens:
                pieces[m, side] = held[m]
                pieces[m | 1, side] = swap(held[m], 1)
        return pieces

    def assemble(pieces, here):
        keys = sorted(pieces)
        rows, cols = pieces[keys[0]].shape
        width = cols // (n_head // 2) // 4
        inner = width * n_head

        def kernel(place_ref, *refs):
            sources, (query_ref, kv_ref, out_ref) = refs[:-3], refs[-3:]
            for (m, side), ref in zip(keys, sources):
                at = pl.ds(pl.multiple_of((place_ref[0] ^ m) * rows, rows), rows)
                for k in range(n_head // 2):
                    s = side * (n_head // 2) + k
                    head = lax.rem(place_ref[1] + n_head - s, n_head)
                    base = k * 4 * width
                    to = pl.ds(pl.multiple_of(head * width, width), width)
                    to_value = pl.ds(pl.multiple_of(inner + head * width, width), width)
                    query_ref[at, to] = ref[:, base : base + width]
                    kv_ref[at, to] = ref[:, base + width : base + 2 * width]
                    kv_ref[at, to_value] = ref[:, base + 2 * width : base + 3 * width]
                    out_ref[at, to] = ref[:, base + 3 * width : base + 4 * width]

        return pl.pallas_call(
            kernel,
            grid_spec=pltpu.PrefetchScalarGridSpec(
                num_scalar_prefetch=1,
                grid=(1,),
                in_specs=[pl.BlockSpec((rows, cols), lambda n, at: (0, 0)) for _ in keys],
                out_specs=[
                    pl.BlockSpec((D, inner), lambda n, at: (0, 0)),
                    pl.BlockSpec((D, 2 * inner), lambda n, at: (0, 0)),
                    pl.BlockSpec((D, inner), lambda n, at: (0, 0)),
                ],
            ),
            out_shape=[jax.ShapeDtypeStruct((D, c), bf16) for c in (inner, 2 * inner, inner)],
            name="assemble",
        )(here, *[pieces[key] for key in keys])

    def assemble_units(pieces, here):
        keys = sorted(pieces)
        rows, cols = pieces[keys[0]].shape
        cols = cols // (n_head // 2)

        def kernel(place_ref, *refs):
            sources, out_ref = refs[:-1], refs[-1]
            for (m, side), ref in zip(keys, sources):
                for k in range(n_head // 2):
                    s = side * (n_head // 2) + k
                    head = lax.rem(place_ref[1] + n_head - s, n_head)
                    at = head * D + (place_ref[0] ^ m) * rows
                    out_ref[pl.ds(pl.multiple_of(at, rows), rows), :] = ref[
                        :, k * cols : (k + 1) * cols
                    ]

        return pl.pallas_call(
            kernel,
            grid_spec=pltpu.PrefetchScalarGridSpec(
                num_scalar_prefetch=1,
                grid=(1,),
                in_specs=[
                    pl.BlockSpec(pieces[key].shape, lambda n, at: (0, 0)) for key in keys
                ],
                out_specs=pl.BlockSpec((n_head * D, cols), lambda n, at: (0, 0)),
            ),
            out_shape=jax.ShapeDtypeStruct((n_head * D, cols), bf16),
            name="assemble_units",
        )(here, *[pieces[key] for key in keys])

    def scatter(keep, send):
        arrived = swap(send, 1)
        _, total_cols = keep.shape
        half = total_cols // 2
        sides = []
        for bits, side in zip(paths, (0, 1)):
            cols = slice(side * half, (side + 1) * half)
            terms = [keep[:, cols], arrived[:, cols]]
            for bit in bits[::-1]:
                middle = terms[0].shape[0] // 2
                away = sum(t[middle:].astype(f32) for t in terms).astype(bf16)
                came = swap(away, bit)
                terms = [t[:middle] for t in terms] + [came]
            sides.append(terms)
        width = total_cols // n_head
        per_side = n_head // 2

        def piece(s):
            at = s % per_side
            cols = slice(at * width, (at + 1) * width)
            return sum(t[:, cols].astype(f32) for t in sides[s // per_side])

        total = piece(0)
        for s in range(1, n_head):
            total = total + shift(piece(s).astype(bf16), n_head - s).astype(f32)
        return total

    def sum_everywhere(values_in):
        steps = [(swap, 1 << b) for b in range(n_dp.bit_length() - 1)]
        steps = steps + [(swap_head, 1 << b) for b in range(n_head.bit_length() - 1)]
        for exchange, bit in steps[:-1]:
            values_in = values_in + exchange(values_in, bit)
        exchange, bit = steps[-1]
        return (values_in, exchange(values_in, bit))

    def place_rows(blocks, here):
        rows, cols = blocks[0].shape

        def kernel(place_ref, *refs):
            away = lax.rem(place_ref[1] + n_head - pl.program_id(0), n_head)
            for s in range(n_head):

                @pl.when(away == s)
                def _(s=s):
                    refs[-1][...] = refs[s][...].astype(f32)

        return pl.pallas_call(
            kernel,
            grid_spec=pltpu.PrefetchScalarGridSpec(
                num_scalar_prefetch=1,
                grid=(n_head,),
                in_specs=[pl.BlockSpec((rows, cols), lambda n, at: (0, 0))] * n_head,
                out_specs=pl.BlockSpec((rows, cols), lambda n, at: (n, 0)),
            ),
            out_shape=jax.ShapeDtypeStruct((n_head * rows, cols), f32),
            name="place_rows",
        )(here, *blocks)

    def share_rows(own, here):
        rows = own.shape[0]
        below, above = [own], [own]
        for _ in range(1, n_head):
            below.append(lax.ppermute(below[-1], "head", [(j, j + 1) for j in range(n_head - 1)]))
            above.append(lax.ppermute(above[-1], "head", [(j, j - 1) for j in range(1, n_head)]))

        def kernel(place_ref, own_ref, *refs):
            lower, upper, out_ref = refs[: n_head - 1], refs[n_head - 1 : -1], refs[-1]
            away = pl.program_id(0) - place_ref[1]

            @pl.when(away == 0)
            def _():
                out_ref[...] = own_ref[...].astype(f32)

            for s in range(1, n_head):

                @pl.when(away == -s)
                def _(s=s):
                    out_ref[...] = lower[s - 1][...].astype(f32)

                @pl.when(away == s)
                def _(s=s):
                    out_ref[...] = upper[s - 1][...].astype(f32)

        one = pl.BlockSpec((rows, D), lambda n, at: (0, 0))
        return pl.pallas_call(
            kernel,
            grid_spec=pltpu.PrefetchScalarGridSpec(
                num_scalar_prefetch=1,
                grid=(n_head,),
                in_specs=[one] * (2 * n_head - 1),
                out_specs=pl.BlockSpec((rows, D), lambda n, at: (n, 0)),
            ),
            out_shape=jax.ShapeDtypeStruct((n_head * rows, D), f32),
            name="share_rows",
        )(here, own, *below[1:], *above[1:])

    def per_device(
        latents,
        media_tokens,
        image_counts,
        time_table,
        media_gain,
        media_bias,
        latent_gain,
        latent_bias,
        feed_gain,
        feed_bias,
        query_weight,
        key_weight,
        value_weight,
        out_weight,
        up_weight,
        down_weight,
        cotangent,
    ):
        me = lax.axis_index("dp")
        my_head = lax.axis_index("head")
        here = jnp.stack([me, my_head]).astype(jnp.int32)
        images_dp = latents.shape[0] // LAT
        images = images_dp // n_head
        lat_rows = images * LAT
        media_rows = images * PATCH

        pieces = gather(
            jnp.concatenate([query_weight, key_weight, value_weight, out_weight.T], axis=1)
        )
        down_turned = down_weight.T
        main = lax.all_gather(
            jnp.concatenate([up_weight[:, EARLY:], down_turned[:, EARLY:]], axis=1),
            ("head", "dp"),
            axis=0,
            tiled=True,
        )
        query_full, kv_full, out_full = assemble(pieces, here)
        extra = assemble_units(
            gather(jnp.concatenate([up_weight[:, :EARLY], down_turned[:, :EARLY]], axis=1)), here
        )

        cot_cols = cotangent.shape[1]
        grad_out = jnp.zeros((lat_rows, D), bf16)
        for s in range(n_head):
            target = (my_head + s) % n_head
            block = lax.dynamic_slice_in_dim(cotangent, target * lat_rows, lat_rows, 0)
            if s:
                block = shift(block, s)
            source = (my_head - s) % n_head
            grad_out = lax.dynamic_update_slice_in_dim(grad_out, block, source * cot_cols, 1)

        first_image = me * images_dp + my_head * images
        counts_sum = jnp.cumsum(image_counts)
        starts = counts_sum - image_counts
        image_index = first_image + jnp.arange(images, dtype=jnp.int32)
        latest = jnp.max(
            jnp.where(starts[None, :] <= image_index[:, None], starts[None, :], 0), axis=1
        )
        media_slots = image_index - latest
        slot_match = media_slots[:, None] == jnp.arange(MAX_MEDIA, dtype=jnp.int32)[None, :]
        per_image = jnp.dot(slot_match.astype(bf16), time_table, preferred_element_type=f32)
        media_own = lax.dynamic_slice_in_dim(media_tokens, my_head * media_rows, media_rows, 0)
        latents_own = lax.dynamic_slice_in_dim(latents, my_head * lat_rows, lat_rows, 0)
        latents_own = latents_own.astype(f32)

        media_sum = (
            media_own.reshape(images, PATCH, D).astype(f32) + per_image[:, None, :]
        ).reshape(media_rows, D)
        media_scaled, _ = norm_stats(media_sum)
        media_norm = (media_scaled * media_gain + media_bias).astype(bf16)
        latent_scaled, latent_inverse = norm_stats(latents_own)
        latent_norm = (latent_scaled * latent_gain + latent_bias).astype(bf16)

        query = mm(latent_norm, query_full).astype(bf16)
        media_kv = mm(media_norm, kv_full).astype(bf16)
        latent_kv = mm(latent_norm, kv_full).astype(bf16)
        mixed = attend(query, media_kv, latent_kv)
        hidden = latents_own + mm_nt(mixed, out_full)
        feed_norm = (norm_stats(hidden)[0] * feed_gain + feed_bias).astype(bf16)

        activation, d_up = hidden_units(feed_norm, grad_out, main, extra)
        down_send = unit_grad(grad_out, activation, here, 1)
        down_keep = unit_grad(grad_out, activation, here, 0)
        down_grad = scatter(down_keep, down_send)
        like = jax.ShapeDtypeStruct
        (result,) = to_features(
            feed_out_kernel, activation, main, extra, 1, [hidden], [like((lat_rows, D), bf16)]
        )
        inner = query_full.shape[1]
        d_hidden, d_attention, d_mixed, feed_gain_part, feed_bias_part = to_features(
            d_feed_kernel,
            d_up,
            main,
            extra,
            0,
            [hidden, grad_out, feed_gain[None, :], out_full],
            [
                like((lat_rows, D), f32),
                like((lat_rows, D), bf16),
                like((lat_rows, inner), bf16),
                like((1, D), f32),
                like((1, D), f32),
            ],
        )

        d_query, d_media_kv, d_latent_kv = attend_back(query, media_kv, latent_kv, d_mixed)
        d_latent_norm = mm_nt(d_query, query_full) + mm_nt(d_latent_kv, kv_full)
        latent_gain_part = jnp.sum(d_latent_norm * latent_scaled, axis=0)
        latent_bias_part = jnp.sum(d_latent_norm, axis=0)
        latent_back = d_hidden + norm_back(
            d_latent_norm, latent_scaled, latent_inverse, latent_gain
        )
        latents_grad = share_rows(latent_back.astype(bf16), here)

        media_gain_part, media_bias_part, image_sums = media_back(
            media_tokens, per_image, media_gain, d_media_kv, kv_full, here
        )
        time_part = jnp.dot(slot_match.astype(f32).T, image_sums, precision=highest)
        small = jnp.concatenate(
            [
                time_part,
                jnp.stack(
                    [
                        media_gain_part,
                        media_bias_part,
                        latent_gain_part,
                        latent_bias_part,
                        feed_gain_part[0],
                        feed_bias_part[0],
                    ]
                ),
            ],
            axis=0,
        )
        small, last_small = sum_everywhere(small)

        d_up, _ = lax.optimization_barrier((d_up, media_gain_part))
        up_send = unit_grad(feed_norm, d_up, here, 1)
        up_keep = unit_grad(feed_norm, d_up, here, 0)
        up_grad = scatter(up_keep, up_send)
        sources = (latent_norm, media_norm, d_attention, d_query, d_media_kv, d_latent_kv, mixed)
        attention_send = attention_grad(*sources, here, 1)
        attention_keep = attention_grad(*sources, here, 0)
        attention_grads = scatter(attention_keep, attention_send)
        last_small, attention_grads = lax.optimization_barrier((last_small, attention_grads))
        small = small + last_small
        width = query_weight.shape[1]
        query_grad, key_grad, value_grad, out_grad = [
            attention_grads[:, at * width : (at + 1) * width] for at in range(4)
        ]

        out_cols = D // n_head
        blocks = []
        for s in range(n_head):
            target = (my_head + s) % n_head
            block = lax.dynamic_slice_in_dim(result, target * out_cols, out_cols, 1)
            if s:
                block = shift(block, s)
            blocks.append(block)
        latents_out = place_rows(blocks, here)
        return (
            latents_out,
            latents_grad,
            small[:MAX_MEDIA],
            small[MAX_MEDIA],
            small[MAX_MEDIA + 1],
            small[MAX_MEDIA + 2],
            small[MAX_MEDIA + 3],
            small[MAX_MEDIA + 4],
            small[MAX_MEDIA + 5],
            query_grad,
            key_grad,
            value_grad,
            out_grad.T,
            jnp.roll(up_grad, EARLY, axis=1),
            jnp.roll(down_grad, EARLY, axis=1).T,
        )

    return per_device


def solution(mesh):
    per_device = make_step(mesh.shape["dp"], mesh.shape["head"])
    rows, both, flipped, whole = P("dp", None), P("dp", "head"), P("head", "dp"), P()
    return jax.shard_map(
        per_device,
        mesh=mesh,
        in_specs=(rows, rows)
        + (whole,) * 8
        + (both, both, both, flipped, both, flipped, both),
        out_specs=(both, rows) + (whole,) * 7 + (both, both, both, flipped, both, flipped),
        check_vma=False,
    )
```

```python
import math

import jax
import jax.numpy as jnp
from jax import lax
from jax.experimental import pallas as pl
from jax.experimental.pallas import tpu as pltpu
from jax.sharding import PartitionSpec as P


D = 1024
DH = 64
LAT = 64
PATCH = 256
MAX_MEDIA = 5
CHUNK = 64
GROUP = 4

epsilon = 1e-05
highest = lax.Precision.HIGHEST
bf16 = jnp.bfloat16
f32 = jnp.float32


def mm(left, right):
    return lax.dot_general(left, right, (((1,), (0,)), ((), ())), preferred_element_type=f32)


def mm_tn(left, right):
    return lax.dot_general(left, right, (((0,), (0,)), ((), ())), preferred_element_type=f32)


def mm_nt(left, right):
    return lax.dot_general(left, right, (((1,), (1,)), ((), ())), preferred_element_type=f32)


def norm_stats(values_in):
    centre = jnp.mean(values_in, axis=-1, keepdims=True)
    shifted = values_in - centre
    spread = jnp.mean(shifted * shifted, axis=-1, keepdims=True)
    inverse = lax.rsqrt(spread + epsilon)
    return (shifted * inverse, inverse)


def norm_back(grad_in, scaled, inverse, norm_gain):
    weighted = grad_in * norm_gain
    return inverse * (
        weighted
        - jnp.mean(weighted, axis=-1, keepdims=True)
        - scaled * jnp.mean(weighted * scaled, axis=-1, keepdims=True)
    )


def gelu_exact(up_proj):
    return up_proj * 0.5 * (1.0 + lax.erf(up_proj * 0.5**0.5))


def gelu_slope(up_proj):
    normal_cdf = 0.5 * (1.0 + lax.erf(up_proj * 0.5**0.5))
    normal_pdf = jnp.exp(-0.5 * up_proj * up_proj) * (2.0 * math.pi) ** (-0.5)
    return normal_cdf + up_proj * normal_pdf


def own_blocks():
    width = GROUP * DH
    rows = lax.broadcasted_iota(jnp.int32, (GROUP * LAT, width), 0) // LAT
    cols = lax.broadcasted_iota(jnp.int32, (GROUP * LAT, width), 1) // DH
    return rows == cols


def spread_heads(block, mask):
    return jnp.where(mask, jnp.concatenate([block] * GROUP, axis=0), jnp.zeros((), block.dtype))


def gather_heads(blocks, mask):
    kept = jnp.where(mask, blocks, 0.0)
    return sum(kept[g * LAT : (g + 1) * LAT] for g in range(GROUP))


def soft_of(query_diag, keys):
    scores = mm_nt(query_diag, keys) * (DH**-0.5)
    expd = jnp.exp(scores - jnp.max(scores, axis=-1, keepdims=True))
    return expd / jnp.sum(expd, axis=-1, keepdims=True)


def attend_kernel(q_ref, km_ref, kl_ref, vm_ref, vl_ref, mixed_ref):
    mask = own_blocks()
    width = GROUP * DH
    for g in range(q_ref.shape[1] // width):
        cols = slice(g * width, (g + 1) * width)
        keys = jnp.concatenate([km_ref[:, cols], kl_ref[:, cols]], axis=0)
        values = jnp.concatenate([vm_ref[:, cols], vl_ref[:, cols]], axis=0)
        soft = soft_of(spread_heads(q_ref[:, cols], mask), keys)
        mixed_ref[:, cols] = gather_heads(mm(soft.astype(bf16), values), mask).astype(bf16)


def attend_back_kernel(
    q_ref, km_ref, kl_ref, vm_ref, vl_ref, dm_ref, dq_ref, dkvm_ref, dkvl_ref
):
    mask = own_blocks()
    width = GROUP * DH
    inner = q_ref.shape[1]
    for g in range(q_ref.shape[1] // width):
        cols = slice(g * width, (g + 1) * width)
        keys = jnp.concatenate([km_ref[:, cols], kl_ref[:, cols]], axis=0)
        values = jnp.concatenate([vm_ref[:, cols], vl_ref[:, cols]], axis=0)
        query_diag = spread_heads(q_ref[:, cols], mask)
        mixed_diag = spread_heads(dm_ref[:, cols], mask)
        soft = soft_of(query_diag, keys)
        d_prob = mm_nt(mixed_diag, values)
        d_value = mm_tn(soft.astype(bf16), mixed_diag).astype(bf16)
        delta = jnp.sum(soft * d_prob, axis=-1, keepdims=True)
        d_scores = (soft * (d_prob - delta)).astype(bf16)
        d_query = gather_heads(mm(d_scores, keys), mask) * (DH**-0.5)
        d_key = (mm_tn(d_scores, query_diag) * (DH**-0.5)).astype(bf16)
        dq_ref[:, cols] = d_query.astype(bf16)
        value_cols = slice(inner + g * width, inner + (g + 1) * width)
        dkvm_ref[:, cols] = d_key[:PATCH]
        dkvl_ref[:, cols] = d_key[PATCH:]
        dkvm_ref[:, value_cols] = d_value[:PATCH]
        dkvl_ref[:, value_cols] = d_value[PATCH:]


def image_spec(rows, cols, block_col=0):
    return pl.BlockSpec((rows, cols), lambda n: (n, block_col))


def attend(query, media_kv, latent_kv):
    inner = query.shape[1]
    images = query.shape[0] // LAT
    return pl.pallas_call(
        attend_kernel,
        grid=(images,),
        in_specs=[
            image_spec(LAT, inner),
            image_spec(PATCH, inner, 0),
            image_spec(LAT, inner, 0),
            image_spec(PATCH, inner, 1),
            image_spec(LAT, inner, 1),
        ],
        out_specs=image_spec(LAT, inner),
        out_shape=jax.ShapeDtypeStruct(query.shape, bf16),
        name="attend",
    )(query, media_kv, latent_kv, media_kv, latent_kv)


def attend_back(query, media_kv, latent_kv, d_mixed):
    inner = query.shape[1]
    images = query.shape[0] // LAT
    return pl.pallas_call(
        attend_back_kernel,
        grid=(images,),
        in_specs=[
            image_spec(LAT, inner),
            image_spec(PATCH, inner, 0),
            image_spec(LAT, inner, 0),
            image_spec(PATCH, inner, 1),
            image_spec(LAT, inner, 1),
            image_spec(LAT, inner),
        ],
        out_specs=[
            image_spec(LAT, inner),
            image_spec(PATCH, 2 * inner),
            image_spec(LAT, 2 * inner),
        ],
        out_shape=[
            jax.ShapeDtypeStruct(shape, bf16)
            for shape in (query.shape, media_kv.shape, latent_kv.shape)
        ],
        name="attend_back",
    )(query, media_kv, latent_kv, media_kv, latent_kv, d_mixed)


EARLY = 256


def unit_specs(main, extra, side):
    return [
        pl.BlockSpec((D, weights.shape[1] // 2), lambda n: (n, side)) for weights in (main, extra)
    ]


def hidden_kernel(norm_ref, grad_ref, up_ref, up_more, down_ref, down_more, act_ref, d_up_ref):
    start = 0
    for up, down in ((up_ref, down_ref), (up_more, down_more)):
        cols = slice(start, start + up.shape[1])
        start += up.shape[1]
        up_proj = mm(norm_ref[...], up[...])
        d_act = mm(grad_ref[...], down[...])
        act_ref[:, cols] = gelu_exact(up_proj).astype(bf16)
        d_up_ref[:, cols] = (d_act * gelu_slope(up_proj)).astype(bf16)


def hidden_units(feed_norm, grad_out, main, extra):
    rows = feed_norm.shape[0]
    n_head = main.shape[0] // D
    per_head = (main.shape[1] + extra.shape[1]) // 2
    units = per_head * n_head
    whole = pl.BlockSpec((rows, D), lambda n: (0, 0))
    cols = pl.BlockSpec((rows, per_head), lambda n: (0, n))
    shape = jax.ShapeDtypeStruct((rows, units), bf16)
    return pl.pallas_call(
        hidden_kernel,
        grid=(n_head,),
        in_specs=[whole, whole] + unit_specs(main, extra, 0) + unit_specs(main, extra, 1),
        out_specs=[cols, cols],
        out_shape=[shape, shape],
        cost_estimate=pl.CostEstimate(
            flops=4 * rows * D * units, bytes_accessed=4 * D * units, transcendentals=rows * units
        ),
        name="hidden_units",
    )(feed_norm, grad_out, main, extra, main, extra)


def add_features(units_ref, weight_ref, more_ref, total):
    @pl.when(pl.program_id(0) == 0)
    def _():
        total[...] = jnp.zeros_like(total)

    split = weight_ref.shape[1]
    total[...] += mm_nt(units_ref[:, :split], weight_ref[...])
    total[...] += mm_nt(units_ref[:, split:], more_ref[...])


def feed_out_kernel(units_ref, weight_ref, more_ref, hidden_ref, out_ref, total):
    add_features(units_ref, weight_ref, more_ref, total)

    @pl.when(pl.program_id(0) == pl.num_programs(0) - 1)
    def _():
        out_ref[...] = (hidden_ref[...] + total[...]).astype(bf16)


def d_feed_kernel(
    units_ref,
    weight_ref,
    more_ref,
    hidden_ref,
    grad_ref,
    gain_ref,
    out_weight_ref,
    d_hidden_ref,
    d_attention_ref,
    d_mixed_ref,
    gain_out,
    bias_out,
    total,
):
    add_features(units_ref, weight_ref, more_ref, total)

    @pl.when(pl.program_id(0) == pl.num_programs(0) - 1)
    def _():
        gain_out[...] = jnp.zeros_like(gain_out)
        bias_out[...] = jnp.zeros_like(bias_out)

        def step(at, carry):
            rows = pl.ds(pl.multiple_of(at * CHUNK, CHUNK), CHUNK)
            d_feed = total[rows, :]
            scaled, inverse = norm_stats(hidden_ref[rows, :])
            gain_out[...] += jnp.sum(d_feed * scaled, axis=0, keepdims=True)
            bias_out[...] += jnp.sum(d_feed, axis=0, keepdims=True)
            d_hidden = grad_ref[rows, :].astype(f32) + norm_back(
                d_feed, scaled, inverse, gain_ref[...]
            )
            d_hidden_ref[rows, :] = d_hidden
            d_attention_ref[rows, :] = d_hidden.astype(bf16)
            return carry

        lax.fori_loop(0, total.shape[0] // CHUNK, step, 0)
        d_mixed_ref[...] = mm(d_attention_ref[...], out_weight_ref[...]).astype(bf16)


def to_features(kernel, units_in, main, extra, side, others, out_shapes):
    rows, units = units_in.shape
    n_head = main.shape[0] // D
    return pl.pallas_call(
        kernel,
        grid=(n_head,),
        in_specs=[pl.BlockSpec((rows, units // n_head), lambda n: (0, n))]
        + unit_specs(main, extra, side)
        + [pl.BlockSpec(other.shape, lambda n: (0, 0)) for other in others],
        out_specs=[pl.BlockSpec(shape.shape, lambda n: (0, 0)) for shape in out_shapes],
        out_shape=out_shapes,
        scratch_shapes=[pltpu.VMEM((rows, D), f32)],
        cost_estimate=pl.CostEstimate(
            flops=2 * rows * D * units, bytes_accessed=2 * D * units, transcendentals=0
        ),
    )(units_in, main, extra, *others)


def media_norm_kernel(place_ref, tokens_ref, added_ref, gain_ref, bias_ref, out_ref):
    def step(at, carry):
        rows = pl.ds(pl.multiple_of(at * CHUNK, CHUNK), CHUNK)
        scaled = norm_stats(tokens_ref[rows, :].astype(f32) + added_ref[0])[0]
        out_ref[rows, :] = (scaled * gain_ref[...] + bias_ref[...]).astype(bf16)
        return carry

    lax.fori_loop(0, PATCH // CHUNK, step, 0)


def media_norm_of(media_tokens, per_image, media_gain, media_bias, here):
    images = per_image.shape[0]
    row = pl.BlockSpec((1, D), lambda n, at: (0, 0))
    return pl.pallas_call(
        media_norm_kernel,
        grid_spec=pltpu.PrefetchScalarGridSpec(
            num_scalar_prefetch=1,
            grid=(images,),
            in_specs=[
                pl.BlockSpec((PATCH, D), lambda n, at: (at[1] * images + n, 0)),
                pl.BlockSpec((1, 1, D), lambda n, at: (n, 0, 0)),
                row,
                row,
            ],
            out_specs=pl.BlockSpec((PATCH, D), lambda n, at: (n, 0)),
        ),
        out_shape=jax.ShapeDtypeStruct((images * PATCH, D), bf16),
        cost_estimate=pl.CostEstimate(
            flops=20 * images * PATCH * D,
            bytes_accessed=4 * images * PATCH * D,
            transcendentals=0,
        ),
        name="media_norm",
    )(here, media_tokens, per_image[:, None, :], media_gain[None, :], media_bias[None, :])


def media_back_kernel(
    place_ref,
    tokens_ref,
    added_ref,
    gain_ref,
    d_kv_ref,
    weight_ref,
    gain_out,
    bias_out,
    sum_out,
):
    @pl.when(pl.program_id(0) == 0)
    def _():
        gain_out[...] = jnp.zeros_like(gain_out)
        bias_out[...] = jnp.zeros_like(bias_out)

    scaled, inverse = norm_stats(tokens_ref[...].astype(f32) + added_ref[0])
    d_norm = mm_nt(d_kv_ref[...], weight_ref[...])
    gain_out[...] += jnp.sum(d_norm * scaled, axis=0, keepdims=True)
    bias_out[...] += jnp.sum(d_norm, axis=0, keepdims=True)
    back = norm_back(d_norm, scaled, inverse, gain_ref[...])
    sum_out[0] = jnp.sum(back, axis=0, keepdims=True)


def media_back(media_tokens, per_image, media_gain, d_media_kv, kv_full, here):
    images = per_image.shape[0]
    row = pl.BlockSpec((1, D), lambda n, at: (0, 0))
    own_row = pl.BlockSpec((1, 1, D), lambda n, at: (n, 0, 0))
    cols = d_media_kv.shape[1]
    gain_sum, bias_sum, sums = pl.pallas_call(
        media_back_kernel,
        grid_spec=pltpu.PrefetchScalarGridSpec(
            num_scalar_prefetch=1,
            grid=(images,),
            in_specs=[
                pl.BlockSpec((PATCH, D), lambda n, at: (at[1] * images + n, 0)),
                own_row,
                row,
                pl.BlockSpec((PATCH, cols), lambda n, at: (n, 0)),
                pl.BlockSpec((D, cols), lambda n, at: (0, 0)),
            ],
            out_specs=[row, row, own_row],
        ),
        out_shape=[
            jax.ShapeDtypeStruct((1, D), f32),
            jax.ShapeDtypeStruct((1, D), f32),
            jax.ShapeDtypeStruct((images, 1, D), f32),
        ],
        cost_estimate=pl.CostEstimate(
            flops=2 * images * PATCH * D * cols,
            bytes_accessed=4 * images * PATCH * D,
            transcendentals=0,
        ),
        name="media_back",
    )(here, media_tokens, per_image[:, None, :], media_gain[None, :], d_media_kv, kv_full)
    return (gain_sum[0], bias_sum[0], sums[:, 0, :])


def join(refs):
    return jnp.concatenate([ref[...] for ref in refs], axis=1)


def unit_grad_kernel(place_ref, *refs):
    left, (right_ref, out_ref) = refs[:-2], refs[-2:]
    out_ref[...] = mm_tn(join(left), right_ref[...]).astype(bf16)


def attention_grad_kernel(place_ref, *refs):
    count = (len(refs) - 7) // 3
    latent, media, attention = refs[:count], refs[count : 2 * count], refs[2 * count : 3 * count]
    dq_ref, dkm_ref, dvm_ref, dkl_ref, dvl_ref, mixed_ref, out_ref = refs[3 * count :]
    latent_rows, media_rows = join(latent), join(media)
    query_part = mm_tn(latent_rows, dq_ref[...])
    kv_part = mm_tn(media_rows, join((dkm_ref, dvm_ref))) + mm_tn(
        latent_rows, join((dkl_ref, dvl_ref))
    )
    out_part = mm_tn(join(attention), mixed_ref[...])
    out_ref[...] = jnp.concatenate([query_part, kv_part, out_part], axis=1).astype(bf16)


def make_step(n_dp, n_head):
    def swap(block, bit):
        return lax.ppermute(block, "dp", [(j, j ^ bit) for j in range(n_dp)])

    def shift(block, step):
        return lax.ppermute(block, "head", [(j, (j + step) % n_head) for j in range(n_head)])

    def swap_head(block, bit):
        return lax.ppermute(block, "head", [(j, j ^ bit) for j in range(n_head)])

    ordered = [1 << b for b in range(1, n_dp.bit_length() - 1)]
    paths = (ordered, ordered[::-1])
    evens = list(range(0, n_dp, 2))
    size = D // n_dp
    wide = size % 128 == 0
    half_blocks = D // 2 // max(size, 128)

    def send_order(bits):
        order = [0]
        for bit in bits:
            order = order + [m | bit for m in order]
        return order

    orders = [send_order(bits) for bits in paths]

    def left_blocks(values_in, me, half, steps):
        rows = values_in.shape[0]
        if wide:
            specs = [
                pl.BlockSpec(
                    (rows, size),
                    lambda n, at, m=m, k=k: (0, at[0] ^ jnp.where(n < steps // 2, m, k)),
                )
                for m, k in zip(*[[m | half for m in order] for order in orders])
            ]
        else:
            parts = [
                lax.dynamic_slice_in_dim(values_in, (me ^ (m | odd)) * size, size, 1)
                for order in orders
                for odd in (0, 1)
                for m in order
            ]
            values_in = jnp.concatenate(parts, axis=1)
            specs = [
                pl.BlockSpec(
                    (rows, 128),
                    lambda n, at, b=b: (0, b + jnp.where(n < steps // 2, 0, D // 128)),
                )
                for b in range(half * half_blocks, (half + 1) * half_blocks)
            ]
        return ([values_in] * half_blocks, specs)

    def unit_grad(left, right, here, half):
        rows, units = right.shape
        block = units // n_head
        operands, specs = left_blocks(left, here[0], half, n_head)
        return pl.pallas_call(
            unit_grad_kernel,
            grid_spec=pltpu.PrefetchScalarGridSpec(
                num_scalar_prefetch=1,
                grid=(n_head,),
                in_specs=specs
                + [
                    pl.BlockSpec(
                        (rows, block), lambda n, at: (0, lax.rem(at[1] + n_head - n, n_head))
                    )
                ],
                out_specs=pl.BlockSpec((D // 2, block), lambda n, at: (0, n)),
            ),
            out_shape=jax.ShapeDtypeStruct((D // 2, units), bf16),
            cost_estimate=pl.CostEstimate(
                flops=rows * D * units, bytes_accessed=D * units, transcendentals=0
            ),
            name="unit_grad",
        )(here, *operands, right)

    def attention_grad(
        latent_norm, media_norm, d_attention, d_query, d_media_kv, d_latent_kv, mixed, here, half
    ):
        inner = d_query.shape[1]
        width = inner // n_head
        operands, specs = [], []
        for left in (latent_norm, media_norm, d_attention):
            more, more_specs = left_blocks(left, here[0], half, n_head)
            operands, specs = operands + more, specs + more_specs

        def group(rows, start):
            return pl.BlockSpec(
                (rows, width), lambda n, at: (0, start + lax.rem(at[1] + n_head - n, n_head))
            )

        lat_rows, media_rows = d_query.shape[0], d_media_kv.shape[0]
        return pl.pallas_call(
            attention_grad_kernel,
            grid_spec=pltpu.PrefetchScalarGridSpec(
                num_scalar_prefetch=1,
                grid=(n_head,),
                in_specs=specs
                + [
                    group(lat_rows, 0),
                    group(media_rows, 0),
                    group(media_rows, n_head),
                    group(lat_rows, 0),
                    group(lat_rows, n_head),
                    group(lat_rows, 0),
                ],
                out_specs=pl.BlockSpec((D // 2, 4 * width), lambda n, at: (0, n)),
            ),
            out_shape=jax.ShapeDtypeStruct((D // 2, 4 * inner), bf16),
            cost_estimate=pl.CostEstimate(
                flops=2 * D * inner * (media_rows + 2 * lat_rows),
                bytes_accessed=4 * D * inner,
                transcendentals=0,
            ),
            name="attention_grad",
        )(here, *operands, d_query, d_media_kv, d_media_kv, d_latent_kv, d_latent_kv, mixed)


    def gather(shard):
        columns = [shard] + [shift(shard, s) for s in range(1, n_head)]
        half = n_head // 2
        pieces = {}
        for side, bits in enumerate(paths):
            held = {0: jnp.concatenate(columns[side * half : (side + 1) * half], axis=1)}
            for bit in bits:
                for m in list(held):
                    held[m | bit] = swap(held[m], bit)
            for m in evens:
                pieces[m, side] = held[m]
                pieces[m | 1, side] = swap(held[m], 1)
        return pieces

    def assemble(pieces, here):
        keys = sorted(pieces)
        rows, cols = pieces[keys[0]].shape
        width = cols // (n_head // 2) // 4
        inner = width * n_head

        def kernel(place_ref, *refs):
            sources, (query_ref, kv_ref, out_ref) = refs[:-3], refs[-3:]
            for (m, side), ref in zip(keys, sources):
                at = pl.ds(pl.multiple_of((place_ref[0] ^ m) * rows, rows), rows)
                for k in range(n_head // 2):
                    s = side * (n_head // 2) + k
                    head = lax.rem(place_ref[1] + n_head - s, n_head)
                    base = k * 4 * width
                    to = pl.ds(pl.multiple_of(head * width, width), width)
                    to_value = pl.ds(pl.multiple_of(inner + head * width, width), width)
                    query_ref[at, to] = ref[:, base : base + width]
                    kv_ref[at, to] = ref[:, base + width : base + 2 * width]
                    kv_ref[at, to_value] = ref[:, base + 2 * width : base + 3 * width]
                    out_ref[at, to] = ref[:, base + 3 * width : base + 4 * width]

        return pl.pallas_call(
            kernel,
            grid_spec=pltpu.PrefetchScalarGridSpec(
                num_scalar_prefetch=1,
                grid=(1,),
                in_specs=[pl.BlockSpec((rows, cols), lambda n, at: (0, 0)) for _ in keys],
                out_specs=[
                    pl.BlockSpec((D, inner), lambda n, at: (0, 0)),
                    pl.BlockSpec((D, 2 * inner), lambda n, at: (0, 0)),
                    pl.BlockSpec((D, inner), lambda n, at: (0, 0)),
                ],
            ),
            out_shape=[jax.ShapeDtypeStruct((D, c), bf16) for c in (inner, 2 * inner, inner)],
            name="assemble",
        )(here, *[pieces[key] for key in keys])

    def assemble_units(pieces, here):
        keys = sorted(pieces)
        rows, cols = pieces[keys[0]].shape
        cols = cols // (n_head // 2)

        def kernel(place_ref, *refs):
            sources, out_ref = refs[:-1], refs[-1]
            for (m, side), ref in zip(keys, sources):
                for k in range(n_head // 2):
                    s = side * (n_head // 2) + k
                    head = lax.rem(place_ref[1] + n_head - s, n_head)
                    at = head * D + (place_ref[0] ^ m) * rows
                    out_ref[pl.ds(pl.multiple_of(at, rows), rows), :] = ref[
                        :, k * cols : (k + 1) * cols
                    ]

        return pl.pallas_call(
            kernel,
            grid_spec=pltpu.PrefetchScalarGridSpec(
                num_scalar_prefetch=1,
                grid=(1,),
                in_specs=[
                    pl.BlockSpec(pieces[key].shape, lambda n, at: (0, 0)) for key in keys
                ],
                out_specs=pl.BlockSpec((n_head * D, cols), lambda n, at: (0, 0)),
            ),
            out_shape=jax.ShapeDtypeStruct((n_head * D, cols), bf16),
            name="assemble_units",
        )(here, *[pieces[key] for key in keys])

    def scatter(keep, send):
        arrived = swap(send, 1)
        _, total_cols = keep.shape
        half = total_cols // 2
        sides = []
        for bits, side in zip(paths, (0, 1)):
            cols = slice(side * half, (side + 1) * half)
            terms = [keep[:, cols], arrived[:, cols]]
            for bit in bits[::-1]:
                middle = terms[0].shape[0] // 2
                away = sum(t[middle:].astype(f32) for t in terms).astype(bf16)
                came = swap(away, bit)
                terms = [t[:middle] for t in terms] + [came]
            sides.append(terms)
        width = total_cols // n_head
        per_side = n_head // 2

        def piece(s):
            at = s % per_side
            cols = slice(at * width, (at + 1) * width)
            return sum(t[:, cols].astype(f32) for t in sides[s // per_side])

        total = piece(0)
        for s in range(1, n_head):
            total = total + shift(piece(s).astype(bf16), n_head - s).astype(f32)
        return total

    def sum_everywhere(values_in, after):
        steps = [(swap, 1 << b) for b in range(n_dp.bit_length() - 1)]
        steps = steps + [(swap_head, 1 << b) for b in range(n_head.bit_length() - 1)]
        for k, (exchange, bit) in enumerate(steps):
            came = exchange(values_in, bit)
            if k >= len(steps) - len(after):
                came, _ = lax.optimization_barrier((came, after[k - len(steps)]))
            values_in = values_in + came
        return values_in

    def place_rows(blocks, here):
        rows, cols = blocks[0].shape

        def kernel(place_ref, *refs):
            away = lax.rem(place_ref[1] + n_head - pl.program_id(0), n_head)
            for s in range(n_head):

                @pl.when(away == s)
                def _(s=s):
                    refs[-1][...] = refs[s][...].astype(f32)

        return pl.pallas_call(
            kernel,
            grid_spec=pltpu.PrefetchScalarGridSpec(
                num_scalar_prefetch=1,
                grid=(n_head,),
                in_specs=[pl.BlockSpec((rows, cols), lambda n, at: (0, 0))] * n_head,
                out_specs=pl.BlockSpec((rows, cols), lambda n, at: (n, 0)),
            ),
            out_shape=jax.ShapeDtypeStruct((n_head * rows, cols), f32),
            name="place_rows",
        )(here, *blocks)

    def per_device(
        latents,
        media_tokens,
        image_counts,
        time_table,
        media_gain,
        media_bias,
        latent_gain,
        latent_bias,
        feed_gain,
        feed_bias,
        query_weight,
        key_weight,
        value_weight,
        out_weight,
        up_weight,
        down_weight,
        cotangent,
    ):
        me = lax.axis_index("dp")
        my_head = lax.axis_index("head")
        here = jnp.stack([me, my_head]).astype(jnp.int32)
        images_dp = latents.shape[0] // LAT
        images = images_dp // n_head
        lat_rows = images * LAT

        pieces = gather(
            jnp.concatenate([query_weight, key_weight, value_weight, out_weight.T], axis=1)
        )
        down_turned = down_weight.T
        main = lax.all_gather(
            jnp.concatenate([up_weight[:, EARLY:], down_turned[:, EARLY:]], axis=1),
            ("head", "dp"),
            axis=0,
            tiled=True,
        )
        query_full, kv_full, out_full = assemble(pieces, here)
        extra = assemble_units(
            gather(jnp.concatenate([up_weight[:, :EARLY], down_turned[:, :EARLY]], axis=1)),
            here,
        )

        cot_cols = cotangent.shape[1]
        grad_out = jnp.zeros((lat_rows, D), bf16)
        for s in range(n_head):
            target = (my_head + s) % n_head
            block = lax.dynamic_slice_in_dim(cotangent, target * lat_rows, lat_rows, 0)
            if s:
                block = shift(block, s)
            source = (my_head - s) % n_head
            grad_out = lax.dynamic_update_slice_in_dim(grad_out, block, source * cot_cols, 1)

        first_image = me * images_dp + my_head * images
        counts_sum = jnp.cumsum(image_counts)
        starts = counts_sum - image_counts
        image_index = first_image + jnp.arange(images, dtype=jnp.int32)
        latest = jnp.max(
            jnp.where(starts[None, :] <= image_index[:, None], starts[None, :], 0), axis=1
        )
        media_slots = image_index - latest
        slot_match = media_slots[:, None] == jnp.arange(MAX_MEDIA, dtype=jnp.int32)[None, :]
        per_image = jnp.dot(slot_match.astype(bf16), time_table, preferred_element_type=f32)
        latents_own = lax.dynamic_slice_in_dim(latents, my_head * lat_rows, lat_rows, 0)
        latents_own = latents_own.astype(f32)

        media_norm = media_norm_of(media_tokens, per_image, media_gain, media_bias, here)
        latent_scaled, latent_inverse = norm_stats(latents_own)
        latent_norm = (latent_scaled * latent_gain + latent_bias).astype(bf16)

        query = mm(latent_norm, query_full).astype(bf16)
        media_kv = mm(media_norm, kv_full).astype(bf16)
        latent_kv = mm(latent_norm, kv_full).astype(bf16)
        mixed = attend(query, media_kv, latent_kv)
        hidden = latents_own + mm_nt(mixed, out_full)
        feed_norm = (norm_stats(hidden)[0] * feed_gain + feed_bias).astype(bf16)

        activation, d_up = hidden_units(feed_norm, grad_out, main, extra)
        down_send = unit_grad(grad_out, activation, here, 1)
        down_keep = unit_grad(grad_out, activation, here, 0)
        down_grad = scatter(down_keep, down_send)
        like = jax.ShapeDtypeStruct
        inner = query_full.shape[1]
        d_hidden, d_attention, d_mixed, feed_gain_part, feed_bias_part = to_features(
            d_feed_kernel,
            d_up,
            main,
            extra,
            0,
            [hidden, grad_out, feed_gain[None, :], out_full],
            [
                like((lat_rows, D), f32),
                like((lat_rows, D), bf16),
                like((lat_rows, inner), bf16),
                like((1, D), f32),
                like((1, D), f32),
            ],
        )

        d_query, d_media_kv, d_latent_kv = attend_back(query, media_kv, latent_kv, d_mixed)
        d_latent_norm = mm_nt(d_query, query_full) + mm_nt(d_latent_kv, kv_full)
        latent_gain_part = jnp.sum(d_latent_norm * latent_scaled, axis=0)
        latent_bias_part = jnp.sum(d_latent_norm, axis=0)
        latent_back = d_hidden + norm_back(
            d_latent_norm, latent_scaled, latent_inverse, latent_gain
        )
        own_grad = latent_back.astype(bf16)
        latents_grad = lax.all_gather(own_grad, "head", axis=0, tiled=True)
        d_up, _ = lax.optimization_barrier((d_up, own_grad))
        up_send = unit_grad(feed_norm, d_up, here, 1)
        up_keep = unit_grad(feed_norm, d_up, here, 0)
        up_grad = scatter(up_keep, up_send)
        activation, _ = lax.optimization_barrier((activation, up_keep))
        (result,) = to_features(
            feed_out_kernel, activation, main, extra, 1, [hidden], [like((lat_rows, D), bf16)]
        )

        media_gain_part, media_bias_part, image_sums = media_back(
            media_tokens, per_image, media_gain, d_media_kv, kv_full, here
        )
        time_part = jnp.dot(slot_match.astype(f32).T, image_sums, precision=highest)
        small = jnp.concatenate(
            [
                time_part,
                jnp.stack(
                    [
                        media_gain_part,
                        media_bias_part,
                        latent_gain_part,
                        latent_bias_part,
                        feed_gain_part[0],
                        feed_bias_part[0],
                    ]
                ),
            ],
            axis=0,
        )

        sources = (latent_norm, media_norm, d_attention, d_query, d_media_kv, d_latent_kv, mixed)
        attention_send = attention_grad(*sources, here, 1)
        attention_keep = attention_grad(*sources, here, 0)
        attention_grads = scatter(attention_keep, attention_send)
        small = sum_everywhere(small, (up_grad, attention_grads))
        latents_grad, _ = lax.optimization_barrier((latents_grad, up_grad))
        latents_grad = latents_grad.astype(f32)
        width = query_weight.shape[1]
        query_grad, key_grad, value_grad, out_grad = [
            attention_grads[:, at * width : (at + 1) * width] for at in range(4)
        ]

        out_cols = D // n_head
        blocks = []
        for s in range(n_head):
            target = (my_head + s) % n_head
            block = lax.dynamic_slice_in_dim(result, target * out_cols, out_cols, 1)
            if s:
                block = shift(block, s)
            blocks.append(block)
        latents_out = place_rows(blocks, here)
        return (
            latents_out,
            latents_grad,
            small[:MAX_MEDIA],
            small[MAX_MEDIA],
            small[MAX_MEDIA + 1],
            small[MAX_MEDIA + 2],
            small[MAX_MEDIA + 3],
            small[MAX_MEDIA + 4],
            small[MAX_MEDIA + 5],
            query_grad,
            key_grad,
            value_grad,
            out_grad.T,
            jnp.roll(up_grad, EARLY, axis=1),
            jnp.roll(down_grad, EARLY, axis=1).T,
        )

    return per_device


def solution(mesh):
    per_device = make_step(mesh.shape["dp"], mesh.shape["head"])
    rows, both, flipped, whole = P("dp", None), P("dp", "head"), P("head", "dp"), P()
    return jax.shard_map(
        per_device,
        mesh=mesh,
        in_specs=(rows, rows)
        + (whole,) * 8
        + (both, both, both, flipped, both, flipped, both),
        out_specs=(both, rows) + (whole,) * 7 + (both, both, both, flipped, both, flipped),
        check_vma=False,
    )
```

```python
import math

import jax
import jax.numpy as jnp
from jax import lax
from jax.experimental import pallas as pl
from jax.experimental.pallas import tpu as pltpu
from jax.sharding import PartitionSpec as P


D = 1024
DH = 64
LAT = 64
PATCH = 256
MAX_MEDIA = 5
CHUNK = 64
GROUP = 4

epsilon = 1e-05
highest = lax.Precision.HIGHEST
bf16 = jnp.bfloat16
f32 = jnp.float32


def mm(left, right):
    return lax.dot_general(left, right, (((1,), (0,)), ((), ())), preferred_element_type=f32)


def mm_tn(left, right):
    return lax.dot_general(left, right, (((0,), (0,)), ((), ())), preferred_element_type=f32)


def mm_nt(left, right):
    return lax.dot_general(left, right, (((1,), (1,)), ((), ())), preferred_element_type=f32)


def norm_stats(values_in):
    centre = jnp.mean(values_in, axis=-1, keepdims=True)
    shifted = values_in - centre
    spread = jnp.mean(shifted * shifted, axis=-1, keepdims=True)
    inverse = lax.rsqrt(spread + epsilon)
    return (shifted * inverse, inverse)


def norm_back(grad_in, scaled, inverse, norm_gain):
    weighted = grad_in * norm_gain
    return inverse * (
        weighted
        - jnp.mean(weighted, axis=-1, keepdims=True)
        - scaled * jnp.mean(weighted * scaled, axis=-1, keepdims=True)
    )


def gelu_exact(up_proj):
    return up_proj * 0.5 * (1.0 + lax.erf(up_proj * 0.5**0.5))


def gelu_slope(up_proj):
    normal_cdf = 0.5 * (1.0 + lax.erf(up_proj * 0.5**0.5))
    normal_pdf = jnp.exp(-0.5 * up_proj * up_proj) * (2.0 * math.pi) ** (-0.5)
    return normal_cdf + up_proj * normal_pdf


def own_blocks():
    width = GROUP * DH
    rows = lax.broadcasted_iota(jnp.int32, (GROUP * LAT, width), 0) // LAT
    cols = lax.broadcasted_iota(jnp.int32, (GROUP * LAT, width), 1) // DH
    return rows == cols


def spread_heads(block, mask):
    return jnp.where(mask, jnp.concatenate([block] * GROUP, axis=0), jnp.zeros((), block.dtype))


def gather_heads(blocks, mask):
    kept = jnp.where(mask, blocks, 0.0)
    return sum(kept[g * LAT : (g + 1) * LAT] for g in range(GROUP))


def soft_of(query_diag, keys):
    scores = mm_nt(query_diag, keys) * (DH**-0.5)
    expd = jnp.exp(scores - jnp.max(scores, axis=-1, keepdims=True))
    return expd / jnp.sum(expd, axis=-1, keepdims=True)


def attend_kernel(q_ref, km_ref, kl_ref, vm_ref, vl_ref, mixed_ref):
    mask = own_blocks()
    width = GROUP * DH
    for g in range(q_ref.shape[1] // width):
        cols = slice(g * width, (g + 1) * width)
        keys = jnp.concatenate([km_ref[:, cols], kl_ref[:, cols]], axis=0)
        values = jnp.concatenate([vm_ref[:, cols], vl_ref[:, cols]], axis=0)
        soft = soft_of(spread_heads(q_ref[:, cols], mask), keys)
        mixed_ref[:, cols] = gather_heads(mm(soft.astype(bf16), values), mask).astype(bf16)


def attend_back_kernel(
    q_ref, km_ref, kl_ref, vm_ref, vl_ref, dm_ref, dq_ref, dkvm_ref, dkvl_ref
):
    mask = own_blocks()
    width = GROUP * DH
    inner = q_ref.shape[1]
    for g in range(q_ref.shape[1] // width):
        cols = slice(g * width, (g + 1) * width)
        keys = jnp.concatenate([km_ref[:, cols], kl_ref[:, cols]], axis=0)
        values = jnp.concatenate([vm_ref[:, cols], vl_ref[:, cols]], axis=0)
        query_diag = spread_heads(q_ref[:, cols], mask)
        mixed_diag = spread_heads(dm_ref[:, cols], mask)
        soft = soft_of(query_diag, keys)
        d_prob = mm_nt(mixed_diag, values)
        d_value = mm_tn(soft.astype(bf16), mixed_diag).astype(bf16)
        delta = jnp.sum(soft * d_prob, axis=-1, keepdims=True)
        d_scores = (soft * (d_prob - delta)).astype(bf16)
        d_query = gather_heads(mm(d_scores, keys), mask) * (DH**-0.5)
        d_key = (mm_tn(d_scores, query_diag) * (DH**-0.5)).astype(bf16)
        dq_ref[:, cols] = d_query.astype(bf16)
        value_cols = slice(inner + g * width, inner + (g + 1) * width)
        dkvm_ref[:, cols] = d_key[:PATCH]
        dkvl_ref[:, cols] = d_key[PATCH:]
        dkvm_ref[:, value_cols] = d_value[:PATCH]
        dkvl_ref[:, value_cols] = d_value[PATCH:]


def image_spec(rows, cols, block_col=0):
    return pl.BlockSpec((rows, cols), lambda n: (n, block_col))


def attend(query, media_kv, latent_kv):
    inner = query.shape[1]
    images = query.shape[0] // LAT
    return pl.pallas_call(
        attend_kernel,
        grid=(images,),
        in_specs=[
            image_spec(LAT, inner),
            image_spec(PATCH, inner, 0),
            image_spec(LAT, inner, 0),
            image_spec(PATCH, inner, 1),
            image_spec(LAT, inner, 1),
        ],
        out_specs=image_spec(LAT, inner),
        out_shape=jax.ShapeDtypeStruct(query.shape, bf16),
        name="attend",
    )(query, media_kv, latent_kv, media_kv, latent_kv)


def attend_back(query, media_kv, latent_kv, d_mixed):
    inner = query.shape[1]
    images = query.shape[0] // LAT
    return pl.pallas_call(
        attend_back_kernel,
        grid=(images,),
        in_specs=[
            image_spec(LAT, inner),
            image_spec(PATCH, inner, 0),
            image_spec(LAT, inner, 0),
            image_spec(PATCH, inner, 1),
            image_spec(LAT, inner, 1),
            image_spec(LAT, inner),
        ],
        out_specs=[
            image_spec(LAT, inner),
            image_spec(PATCH, 2 * inner),
            image_spec(LAT, 2 * inner),
        ],
        out_shape=[
            jax.ShapeDtypeStruct(shape, bf16)
            for shape in (query.shape, media_kv.shape, latent_kv.shape)
        ],
        name="attend_back",
    )(query, media_kv, latent_kv, media_kv, latent_kv, d_mixed)


EARLY = 256


def unit_specs(main, extra, side):
    return [
        pl.BlockSpec((D, weights.shape[1] // 2), lambda n: (n, side)) for weights in (main, extra)
    ]


def hidden_kernel(norm_ref, grad_ref, up_ref, up_more, down_ref, down_more, act_ref, d_up_ref):
    start = 0
    for up, down in ((up_ref, down_ref), (up_more, down_more)):
        cols = slice(start, start + up.shape[1])
        start += up.shape[1]
        up_proj = mm(norm_ref[...], up[...])
        d_act = mm(grad_ref[...], down[...])
        act_ref[:, cols] = gelu_exact(up_proj).astype(bf16)
        d_up_ref[:, cols] = (d_act * gelu_slope(up_proj)).astype(bf16)


def hidden_units(feed_norm, grad_out, main, extra):
    rows = feed_norm.shape[0]
    n_head = main.shape[0] // D
    per_head = (main.shape[1] + extra.shape[1]) // 2
    units = per_head * n_head
    whole = pl.BlockSpec((rows, D), lambda n: (0, 0))
    cols = pl.BlockSpec((rows, per_head), lambda n: (0, n))
    shape = jax.ShapeDtypeStruct((rows, units), bf16)
    return pl.pallas_call(
        hidden_kernel,
        grid=(n_head,),
        in_specs=[whole, whole] + unit_specs(main, extra, 0) + unit_specs(main, extra, 1),
        out_specs=[cols, cols],
        out_shape=[shape, shape],
        cost_estimate=pl.CostEstimate(
            flops=4 * rows * D * units, bytes_accessed=4 * D * units, transcendentals=rows * units
        ),
        name="hidden_units",
    )(feed_norm, grad_out, main, extra, main, extra)


def add_features(units_ref, weight_ref, more_ref, total):
    @pl.when(pl.program_id(0) == 0)
    def _():
        total[...] = jnp.zeros_like(total)

    split = weight_ref.shape[1]
    total[...] += mm_nt(units_ref[:, :split], weight_ref[...])
    total[...] += mm_nt(units_ref[:, split:], more_ref[...])


def feed_out_kernel(units_ref, weight_ref, more_ref, hidden_ref, out_ref, total):
    add_features(units_ref, weight_ref, more_ref, total)

    @pl.when(pl.program_id(0) == pl.num_programs(0) - 1)
    def _():
        out_ref[...] = (hidden_ref[...] + total[...]).astype(bf16)


def d_feed_kernel(
    units_ref,
    weight_ref,
    more_ref,
    hidden_ref,
    grad_ref,
    gain_ref,
    out_weight_ref,
    d_hidden_ref,
    d_attention_ref,
    d_mixed_ref,
    gain_out,
    bias_out,
    total,
):
    add_features(units_ref, weight_ref, more_ref, total)

    @pl.when(pl.program_id(0) == pl.num_programs(0) - 1)
    def _():
        gain_out[...] = jnp.zeros_like(gain_out)
        bias_out[...] = jnp.zeros_like(bias_out)

        def step(at, carry):
            rows = pl.ds(pl.multiple_of(at * CHUNK, CHUNK), CHUNK)
            d_feed = total[rows, :]
            scaled, inverse = norm_stats(hidden_ref[rows, :])
            gain_out[...] += jnp.sum(d_feed * scaled, axis=0, keepdims=True)
            bias_out[...] += jnp.sum(d_feed, axis=0, keepdims=True)
            d_hidden = grad_ref[rows, :].astype(f32) + norm_back(
                d_feed, scaled, inverse, gain_ref[...]
            )
            d_hidden_ref[rows, :] = d_hidden
            d_attention_ref[rows, :] = d_hidden.astype(bf16)
            return carry

        lax.fori_loop(0, total.shape[0] // CHUNK, step, 0)
        d_mixed_ref[...] = mm(d_attention_ref[...], out_weight_ref[...]).astype(bf16)


def to_features(kernel, units_in, main, extra, side, others, out_shapes):
    rows, units = units_in.shape
    n_head = main.shape[0] // D
    return pl.pallas_call(
        kernel,
        grid=(n_head,),
        in_specs=[pl.BlockSpec((rows, units // n_head), lambda n: (0, n))]
        + unit_specs(main, extra, side)
        + [pl.BlockSpec(other.shape, lambda n: (0, 0)) for other in others],
        out_specs=[pl.BlockSpec(shape.shape, lambda n: (0, 0)) for shape in out_shapes],
        out_shape=out_shapes,
        scratch_shapes=[pltpu.VMEM((rows, D), f32)],
        cost_estimate=pl.CostEstimate(
            flops=2 * rows * D * units, bytes_accessed=2 * D * units, transcendentals=0
        ),
    )(units_in, main, extra, *others)


def media_norm_kernel(place_ref, tokens_ref, added_ref, gain_ref, bias_ref, out_ref):
    def step(at, carry):
        rows = pl.ds(pl.multiple_of(at * CHUNK, CHUNK), CHUNK)
        scaled = norm_stats(tokens_ref[rows, :].astype(f32) + added_ref[0])[0]
        out_ref[rows, :] = (scaled * gain_ref[...] + bias_ref[...]).astype(bf16)
        return carry

    lax.fori_loop(0, PATCH // CHUNK, step, 0)


def media_norm_of(media_tokens, per_image, media_gain, media_bias, here):
    images = per_image.shape[0]
    row = pl.BlockSpec((1, D), lambda n, at: (0, 0))
    return pl.pallas_call(
        media_norm_kernel,
        grid_spec=pltpu.PrefetchScalarGridSpec(
            num_scalar_prefetch=1,
            grid=(images,),
            in_specs=[
                pl.BlockSpec((PATCH, D), lambda n, at: (at[1] * images + n, 0)),
                pl.BlockSpec((1, 1, D), lambda n, at: (n, 0, 0)),
                row,
                row,
            ],
            out_specs=pl.BlockSpec((PATCH, D), lambda n, at: (n, 0)),
        ),
        out_shape=jax.ShapeDtypeStruct((images * PATCH, D), bf16),
        cost_estimate=pl.CostEstimate(
            flops=20 * images * PATCH * D,
            bytes_accessed=4 * images * PATCH * D,
            transcendentals=0,
        ),
        name="media_norm",
    )(here, media_tokens, per_image[:, None, :], media_gain[None, :], media_bias[None, :])


def media_back_kernel(
    place_ref,
    tokens_ref,
    added_ref,
    gain_ref,
    d_kv_ref,
    weight_ref,
    gain_out,
    bias_out,
    sum_out,
):
    @pl.when(pl.program_id(0) == 0)
    def _():
        gain_out[...] = jnp.zeros_like(gain_out)
        bias_out[...] = jnp.zeros_like(bias_out)

    scaled, inverse = norm_stats(tokens_ref[...].astype(f32) + added_ref[0])
    d_norm = mm_nt(d_kv_ref[...], weight_ref[...])
    gain_out[...] += jnp.sum(d_norm * scaled, axis=0, keepdims=True)
    bias_out[...] += jnp.sum(d_norm, axis=0, keepdims=True)
    back = norm_back(d_norm, scaled, inverse, gain_ref[...])
    sum_out[0] = jnp.sum(back, axis=0, keepdims=True)


def media_back(media_tokens, per_image, media_gain, d_media_kv, kv_full, here):
    images = per_image.shape[0]
    row = pl.BlockSpec((1, D), lambda n, at: (0, 0))
    own_row = pl.BlockSpec((1, 1, D), lambda n, at: (n, 0, 0))
    cols = d_media_kv.shape[1]
    gain_sum, bias_sum, sums = pl.pallas_call(
        media_back_kernel,
        grid_spec=pltpu.PrefetchScalarGridSpec(
            num_scalar_prefetch=1,
            grid=(images,),
            in_specs=[
                pl.BlockSpec((PATCH, D), lambda n, at: (at[1] * images + n, 0)),
                own_row,
                row,
                pl.BlockSpec((PATCH, cols), lambda n, at: (n, 0)),
                pl.BlockSpec((D, cols), lambda n, at: (0, 0)),
            ],
            out_specs=[row, row, own_row],
        ),
        out_shape=[
            jax.ShapeDtypeStruct((1, D), f32),
            jax.ShapeDtypeStruct((1, D), f32),
            jax.ShapeDtypeStruct((images, 1, D), f32),
        ],
        cost_estimate=pl.CostEstimate(
            flops=2 * images * PATCH * D * cols,
            bytes_accessed=4 * images * PATCH * D,
            transcendentals=0,
        ),
        name="media_back",
    )(here, media_tokens, per_image[:, None, :], media_gain[None, :], d_media_kv, kv_full)
    return (gain_sum[0], bias_sum[0], sums[:, 0, :])


def join(refs):
    return jnp.concatenate([ref[...] for ref in refs], axis=1)


def unit_grad_kernel(place_ref, *refs):
    left, (right_ref, out_ref) = refs[:-2], refs[-2:]
    out_ref[...] = mm_tn(join(left), right_ref[...]).astype(bf16)


def attention_grad_kernel(place_ref, *refs):
    count = (len(refs) - 7) // 3
    latent, media, attention = refs[:count], refs[count : 2 * count], refs[2 * count : 3 * count]
    dq_ref, dkm_ref, dvm_ref, dkl_ref, dvl_ref, mixed_ref, out_ref = refs[3 * count :]
    latent_rows, media_rows = join(latent), join(media)
    query_part = mm_tn(latent_rows, dq_ref[...])
    kv_part = mm_tn(media_rows, join((dkm_ref, dvm_ref))) + mm_tn(
        latent_rows, join((dkl_ref, dvl_ref))
    )
    out_part = mm_tn(join(attention), mixed_ref[...])
    out_ref[...] = jnp.concatenate([query_part, kv_part, out_part], axis=1).astype(bf16)


def make_step(n_dp, n_head):
    def swap(block, bit):
        return lax.ppermute(block, "dp", [(j, j ^ bit) for j in range(n_dp)])

    def shift(block, step):
        return lax.ppermute(block, "head", [(j, (j + step) % n_head) for j in range(n_head)])

    def swap_head(block, bit):
        return lax.ppermute(block, "head", [(j, j ^ bit) for j in range(n_head)])

    ordered = [1 << b for b in range(1, n_dp.bit_length() - 1)]
    paths = (ordered, ordered[::-1])
    evens = list(range(0, n_dp, 2))
    size = D // n_dp
    wide = size % 128 == 0
    half_blocks = D // 2 // max(size, 128)

    def send_order(bits):
        order = [0]
        for bit in bits:
            order = order + [m | bit for m in order]
        return order

    orders = [send_order(bits) for bits in paths]

    def left_blocks(values_in, me, half, steps):
        rows = values_in.shape[0]
        if wide:
            specs = [
                pl.BlockSpec(
                    (rows, size),
                    lambda n, at, m=m, k=k: (0, at[0] ^ jnp.where(n < steps // 2, m, k)),
                )
                for m, k in zip(*[[m | half for m in order] for order in orders])
            ]
        else:
            parts = [
                lax.dynamic_slice_in_dim(values_in, (me ^ (m | odd)) * size, size, 1)
                for order in orders
                for odd in (0, 1)
                for m in order
            ]
            values_in = jnp.concatenate(parts, axis=1)
            specs = [
                pl.BlockSpec(
                    (rows, 128),
                    lambda n, at, b=b: (0, b + jnp.where(n < steps // 2, 0, D // 128)),
                )
                for b in range(half * half_blocks, (half + 1) * half_blocks)
            ]
        return ([values_in] * half_blocks, specs)

    def unit_grad(left, right, here, half):
        rows, units = right.shape
        block = units // n_head
        operands, specs = left_blocks(left, here[0], half, n_head)
        return pl.pallas_call(
            unit_grad_kernel,
            grid_spec=pltpu.PrefetchScalarGridSpec(
                num_scalar_prefetch=1,
                grid=(n_head,),
                in_specs=specs
                + [
                    pl.BlockSpec(
                        (rows, block), lambda n, at: (0, lax.rem(at[1] + n_head - n, n_head))
                    )
                ],
                out_specs=pl.BlockSpec((D // 2, block), lambda n, at: (0, n)),
            ),
            out_shape=jax.ShapeDtypeStruct((D // 2, units), bf16),
            cost_estimate=pl.CostEstimate(
                flops=rows * D * units, bytes_accessed=D * units, transcendentals=0
            ),
            name="unit_grad",
        )(here, *operands, right)

    def attention_grad(
        latent_norm, media_norm, d_attention, d_query, d_media_kv, d_latent_kv, mixed, here, half
    ):
        inner = d_query.shape[1]
        width = inner // n_head
        operands, specs = [], []
        for left in (latent_norm, media_norm, d_attention):
            more, more_specs = left_blocks(left, here[0], half, n_head)
            operands, specs = operands + more, specs + more_specs

        def group(rows, start):
            return pl.BlockSpec(
                (rows, width), lambda n, at: (0, start + lax.rem(at[1] + n_head - n, n_head))
            )

        lat_rows, media_rows = d_query.shape[0], d_media_kv.shape[0]
        return pl.pallas_call(
            attention_grad_kernel,
            grid_spec=pltpu.PrefetchScalarGridSpec(
                num_scalar_prefetch=1,
                grid=(n_head,),
                in_specs=specs
                + [
                    group(lat_rows, 0),
                    group(media_rows, 0),
                    group(media_rows, n_head),
                    group(lat_rows, 0),
                    group(lat_rows, n_head),
                    group(lat_rows, 0),
                ],
                out_specs=pl.BlockSpec((D // 2, 4 * width), lambda n, at: (0, n)),
            ),
            out_shape=jax.ShapeDtypeStruct((D // 2, 4 * inner), bf16),
            cost_estimate=pl.CostEstimate(
                flops=2 * D * inner * (media_rows + 2 * lat_rows),
                bytes_accessed=4 * D * inner,
                transcendentals=0,
            ),
            name="attention_grad",
        )(here, *operands, d_query, d_media_kv, d_media_kv, d_latent_kv, d_latent_kv, mixed)


    def gather(shard):
        columns = [shard] + [shift(shard, s) for s in range(1, n_head)]
        half = n_head // 2
        pieces = {}
        for side, bits in enumerate(paths):
            held = {0: jnp.concatenate(columns[side * half : (side + 1) * half], axis=1)}
            for bit in bits:
                for m in list(held):
                    held[m | bit] = swap(held[m], bit)
            for m in evens:
                pieces[m, side] = held[m]
                pieces[m | 1, side] = swap(held[m], 1)
        return pieces

    def assemble(pieces, here):
        keys = sorted(pieces)
        rows, cols = pieces[keys[0]].shape
        width = cols // (n_head // 2) // 4
        inner = width * n_head

        def kernel(place_ref, *refs):
            sources, (query_ref, kv_ref, out_ref) = refs[:-3], refs[-3:]
            for (m, side), ref in zip(keys, sources):
                at = pl.ds(pl.multiple_of((place_ref[0] ^ m) * rows, rows), rows)
                for k in range(n_head // 2):
                    s = side * (n_head // 2) + k
                    head = lax.rem(place_ref[1] + n_head - s, n_head)
                    base = k * 4 * width
                    to = pl.ds(pl.multiple_of(head * width, width), width)
                    to_value = pl.ds(pl.multiple_of(inner + head * width, width), width)
                    query_ref[at, to] = ref[:, base : base + width]
                    kv_ref[at, to] = ref[:, base + width : base + 2 * width]
                    kv_ref[at, to_value] = ref[:, base + 2 * width : base + 3 * width]
                    out_ref[at, to] = ref[:, base + 3 * width : base + 4 * width]

        return pl.pallas_call(
            kernel,
            grid_spec=pltpu.PrefetchScalarGridSpec(
                num_scalar_prefetch=1,
                grid=(1,),
                in_specs=[pl.BlockSpec((rows, cols), lambda n, at: (0, 0)) for _ in keys],
                out_specs=[
                    pl.BlockSpec((D, inner), lambda n, at: (0, 0)),
                    pl.BlockSpec((D, 2 * inner), lambda n, at: (0, 0)),
                    pl.BlockSpec((D, inner), lambda n, at: (0, 0)),
                ],
            ),
            out_shape=[jax.ShapeDtypeStruct((D, c), bf16) for c in (inner, 2 * inner, inner)],
            name="assemble",
        )(here, *[pieces[key] for key in keys])

    def assemble_units(pieces, here):
        keys = sorted(pieces)
        rows, cols = pieces[keys[0]].shape
        cols = cols // (n_head // 2)

        def kernel(place_ref, *refs):
            sources, out_ref = refs[:-1], refs[-1]
            for (m, side), ref in zip(keys, sources):
                for k in range(n_head // 2):
                    s = side * (n_head // 2) + k
                    head = lax.rem(place_ref[1] + n_head - s, n_head)
                    at = head * D + (place_ref[0] ^ m) * rows
                    out_ref[pl.ds(pl.multiple_of(at, rows), rows), :] = ref[
                        :, k * cols : (k + 1) * cols
                    ]

        return pl.pallas_call(
            kernel,
            grid_spec=pltpu.PrefetchScalarGridSpec(
                num_scalar_prefetch=1,
                grid=(1,),
                in_specs=[
                    pl.BlockSpec(pieces[key].shape, lambda n, at: (0, 0)) for key in keys
                ],
                out_specs=pl.BlockSpec((n_head * D, cols), lambda n, at: (0, 0)),
            ),
            out_shape=jax.ShapeDtypeStruct((n_head * D, cols), bf16),
            name="assemble_units",
        )(here, *[pieces[key] for key in keys])

    def scatter(keep, send):
        arrived = swap(send, 1)
        _, total_cols = keep.shape
        half = total_cols // 2
        sides = []
        for bits, side in zip(paths, (0, 1)):
            cols = slice(side * half, (side + 1) * half)
            terms = [keep[:, cols], arrived[:, cols]]
            for bit in bits[::-1]:
                middle = terms[0].shape[0] // 2
                away = sum(t[middle:].astype(f32) for t in terms).astype(bf16)
                came = swap(away, bit)
                terms = [t[:middle] for t in terms] + [came]
            sides.append(terms)
        width = total_cols // n_head
        per_side = n_head // 2

        def piece(s):
            at = s % per_side
            cols = slice(at * width, (at + 1) * width)
            return sum(t[:, cols].astype(f32) for t in sides[s // per_side])

        total = piece(0)
        for s in range(1, n_head):
            total = total + shift(piece(s).astype(bf16), n_head - s).astype(f32)
        return total

    def sum_everywhere(values_in, after):
        steps = [(swap, 1 << b) for b in range(n_dp.bit_length() - 1)]
        steps = steps + [(swap_head, 1 << b) for b in range(n_head.bit_length() - 1)]
        for k, (exchange, bit) in enumerate(steps):
            came = exchange(values_in, bit)
            if k >= len(steps) - len(after):
                came, _ = lax.optimization_barrier((came, after[k - len(steps)]))
            values_in = values_in + came
        return values_in

    def place_rows(blocks, here):
        rows, cols = blocks[0].shape

        def kernel(place_ref, *refs):
            away = lax.rem(place_ref[1] + n_head - pl.program_id(0), n_head)
            for s in range(n_head):

                @pl.when(away == s)
                def _(s=s):
                    refs[-1][...] = refs[s][...].astype(f32)

        return pl.pallas_call(
            kernel,
            grid_spec=pltpu.PrefetchScalarGridSpec(
                num_scalar_prefetch=1,
                grid=(n_head,),
                in_specs=[pl.BlockSpec((rows, cols), lambda n, at: (0, 0))] * n_head,
                out_specs=pl.BlockSpec((rows, cols), lambda n, at: (n, 0)),
            ),
            out_shape=jax.ShapeDtypeStruct((n_head * rows, cols), f32),
            name="place_rows",
        )(here, *blocks)

    def per_device(
        latents,
        media_tokens,
        image_counts,
        time_table,
        media_gain,
        media_bias,
        latent_gain,
        latent_bias,
        feed_gain,
        feed_bias,
        query_weight,
        key_weight,
        value_weight,
        out_weight,
        up_weight,
        down_weight,
        cotangent,
    ):
        me = lax.axis_index("dp")
        my_head = lax.axis_index("head")
        here = jnp.stack([me, my_head]).astype(jnp.int32)
        images_dp = latents.shape[0] // LAT
        images = images_dp // n_head
        lat_rows = images * LAT

        pieces = gather(
            jnp.concatenate([query_weight, key_weight, value_weight, out_weight.T], axis=1)
        )
        down_turned = down_weight.T
        main = lax.all_gather(
            jnp.concatenate([up_weight[:, EARLY:], down_turned[:, EARLY:]], axis=1),
            ("head", "dp"),
            axis=0,
            tiled=True,
        )
        query_full, kv_full, out_full = assemble(pieces, here)
        extra = assemble_units(
            gather(jnp.concatenate([up_weight[:, :EARLY], down_turned[:, :EARLY]], axis=1)),
            here,
        )

        cot_cols = cotangent.shape[1]
        grad_out = jnp.zeros((lat_rows, D), bf16)
        for s in range(n_head):
            target = (my_head + s) % n_head
            block = lax.dynamic_slice_in_dim(cotangent, target * lat_rows, lat_rows, 0)
            if s:
                block = shift(block, s)
            source = (my_head - s) % n_head
            grad_out = lax.dynamic_update_slice_in_dim(grad_out, block, source * cot_cols, 1)

        first_image = me * images_dp + my_head * images
        counts_sum = jnp.cumsum(image_counts)
        starts = counts_sum - image_counts
        image_index = first_image + jnp.arange(images, dtype=jnp.int32)
        latest = jnp.max(
            jnp.where(starts[None, :] <= image_index[:, None], starts[None, :], 0), axis=1
        )
        media_slots = image_index - latest
        slot_match = media_slots[:, None] == jnp.arange(MAX_MEDIA, dtype=jnp.int32)[None, :]
        per_image = jnp.dot(slot_match.astype(bf16), time_table, preferred_element_type=f32)
        latents_own = lax.dynamic_slice_in_dim(latents, my_head * lat_rows, lat_rows, 0)
        latents_own = latents_own.astype(f32)

        media_norm = media_norm_of(media_tokens, per_image, media_gain, media_bias, here)
        latent_scaled, latent_inverse = norm_stats(latents_own)
        latent_norm = (latent_scaled * latent_gain + latent_bias).astype(bf16)

        query = mm(latent_norm, query_full).astype(bf16)
        media_kv = mm(media_norm, kv_full).astype(bf16)
        latent_kv = mm(latent_norm, kv_full).astype(bf16)
        mixed = attend(query, media_kv, latent_kv)
        hidden = latents_own + mm_nt(mixed, out_full)
        feed_norm = (norm_stats(hidden)[0] * feed_gain + feed_bias).astype(bf16)

        activation, d_up = hidden_units(feed_norm, grad_out, main, extra)
        like = jax.ShapeDtypeStruct
        inner = query_full.shape[1]
        d_hidden, d_attention, d_mixed, feed_gain_part, feed_bias_part = to_features(
            d_feed_kernel,
            d_up,
            main,
            extra,
            0,
            [hidden, grad_out, feed_gain[None, :], out_full],
            [
                like((lat_rows, D), f32),
                like((lat_rows, D), bf16),
                like((lat_rows, inner), bf16),
                like((1, D), f32),
                like((1, D), f32),
            ],
        )

        d_query, d_media_kv, d_latent_kv = attend_back(query, media_kv, latent_kv, d_mixed)
        d_latent_norm = mm_nt(d_query, query_full) + mm_nt(d_latent_kv, kv_full)
        latent_gain_part = jnp.sum(d_latent_norm * latent_scaled, axis=0)
        latent_bias_part = jnp.sum(d_latent_norm, axis=0)
        latent_back = d_hidden + norm_back(
            d_latent_norm, latent_scaled, latent_inverse, latent_gain
        )
        own_grad = latent_back.astype(bf16)
        latents_grad = lax.all_gather(own_grad, "head", axis=0, tiled=True)
        activation, d_up, _ = lax.optimization_barrier((activation, d_up, own_grad))
        down_send = unit_grad(grad_out, activation, here, 1)
        down_keep = unit_grad(grad_out, activation, here, 0)
        down_grad = scatter(down_keep, down_send)
        up_send = unit_grad(feed_norm, d_up, here, 1)
        up_keep = unit_grad(feed_norm, d_up, here, 0)
        up_grad = scatter(up_keep, up_send)
        activation, _ = lax.optimization_barrier((activation, up_keep))
        (result,) = to_features(
            feed_out_kernel, activation, main, extra, 1, [hidden], [like((lat_rows, D), bf16)]
        )

        media_gain_part, media_bias_part, image_sums = media_back(
            media_tokens, per_image, media_gain, d_media_kv, kv_full, here
        )
        time_part = jnp.dot(slot_match.astype(f32).T, image_sums, precision=highest)
        small = jnp.concatenate(
            [
                time_part,
                jnp.stack(
                    [
                        media_gain_part,
                        media_bias_part,
                        latent_gain_part,
                        latent_bias_part,
                        feed_gain_part[0],
                        feed_bias_part[0],
                    ]
                ),
            ],
            axis=0,
        )

        sources = (latent_norm, media_norm, d_attention, d_query, d_media_kv, d_latent_kv, mixed)
        attention_send = attention_grad(*sources, here, 1)
        attention_keep = attention_grad(*sources, here, 0)
        attention_grads = scatter(attention_keep, attention_send)
        small = sum_everywhere(small, (up_grad, attention_grads))
        latents_grad, _ = lax.optimization_barrier((latents_grad, down_grad))
        latents_grad = latents_grad.astype(f32)
        width = query_weight.shape[1]
        query_grad, key_grad, value_grad, out_grad = [
            attention_grads[:, at * width : (at + 1) * width] for at in range(4)
        ]

        out_cols = D // n_head
        blocks = []
        for s in range(n_head):
            target = (my_head + s) % n_head
            block = lax.dynamic_slice_in_dim(result, target * out_cols, out_cols, 1)
            if s:
                block = shift(block, s)
            blocks.append(block)
        blocks, _ = lax.optimization_barrier((blocks, down_grad))
        latents_out = place_rows(blocks, here)
        return (
            latents_out,
            latents_grad,
            small[:MAX_MEDIA],
            small[MAX_MEDIA],
            small[MAX_MEDIA + 1],
            small[MAX_MEDIA + 2],
            small[MAX_MEDIA + 3],
            small[MAX_MEDIA + 4],
            small[MAX_MEDIA + 5],
            query_grad,
            key_grad,
            value_grad,
            out_grad.T,
            jnp.roll(up_grad, EARLY, axis=1),
            jnp.roll(down_grad, EARLY, axis=1).T,
        )

    return per_device


def solution(mesh):
    per_device = make_step(mesh.shape["dp"], mesh.shape["head"])
    rows, both, flipped, whole = P("dp", None), P("dp", "head"), P("head", "dp"), P()
    return jax.shard_map(
        per_device,
        mesh=mesh,
        in_specs=(rows, rows)
        + (whole,) * 8
        + (both, both, both, flipped, both, flipped, both),
        out_specs=(both, rows) + (whole,) * 7 + (both, both, both, flipped, both, flipped),
        check_vma=False,
    )
```
